128 devices in a mesh: tm: 4 (over x_hi, core), gx: 8 (over x_lo, y), gy: 4 (over z).
Axes of the slice: x: 4 (x_hi: 2, x_lo: 2; x = x_hi * 2 + x_lo), y: 4, z: 4, core: 2. Of those that a mesh axis runs over, the one named last changes fastest.
Arguments:
- velocity: float32 [3, 128, 128, 256], P(None, 'gx', 'gy'), may hold values from -3 to 3
- start_field: float32 [3, 128, 128, 256], P(None, 'gx', 'gy'), may hold values from -6 to 6
- guess: float32 [4, 3, 128, 128, 256], P('tm', None, 'gx', 'gy'), may hold values from -6 to 6
Outputs:
- slab_ends: float32 [4, 3, 128, 128, 256], P('tm', None, 'gx', 'gy')
The draws below stay inside these ranges and needn't reach their ends.
All inputs are finite; a program needn't handle non-finite values.
Results may differ from the reference program's by a relative error of at most 0.0003.
Values sent between devices are 32-bit elements; how exact they have to be, the bound alone decides.
A program may use at most 128 MiB of HBM per device.

```python
import jax
import jax.numpy as jnp

NZ = 256
ITERS = 2
SLABS = 4
NX = 128
NY = 128


def block_levels(own_key, dims, cuts, smallest, largest):
    loudness, own = 1.0, jax.random.fold_in(own_key, 6)
    for axis_at, shards_of in cuts:
        draws = jnp.exp(jax.random.uniform(jax.random.fold_in(own, axis_at), (shards_of,), jnp.float32, smallest / len(cuts), largest / len(cuts)))
        loudness = loudness * jnp.repeat(draws, dims[axis_at] // shards_of).reshape([-1 if axis == axis_at else 1 for axis in range(len(dims))])
    return loudness


def centred(own_key, dims, scale, bound, cuts=(), held_as=jnp.bfloat16):
    level = block_levels(own_key, dims, cuts, -0.22, 0.18) if cuts else 1.0
    values = jax.random.normal(own_key, dims, jnp.float32) * scale * level
    return jnp.minimum(jnp.maximum(values, -bound), bound).astype(held_as)


def setup_inputs(seed: int = 0) -> dict:
    seeds = jax.random.split(jax.random.key(seed), 4)
    return {
        "velocity": centred(seeds[0], (3, NX, NY, NZ), 0.5, 3.0, ((1, 8), (2, 4)), jnp.float32),
        "start_field": centred(seeds[1], (3, NX, NY, NZ), 1.0, 6.0, ((1, 8), (2, 4)), jnp.float32),
        "guess": centred(seeds[2], (SLABS, 3, NX, NY, NZ), 1.0, 6.0, ((0, 4), (2, 8), (3, 4)), jnp.float32),
    }


VISCOSITY = 0.25
TIME_STEP = 0.5


def gradients(velocity):
    rows = []
    for target in range(3):
        for across in range(3):
            ahead = jnp.roll(velocity[target], -1, across)
            behind = jnp.roll(velocity[target], 1, across)
            rows.append((ahead - behind) / 2.0)
    return jnp.stack(rows)


def restrict(field):
    extent = field.shape
    blocks = field.reshape(extent[0], extent[1] // 2, 2, extent[2] // 2, 2, extent[3] // 2, 2)
    return jnp.mean(blocks, axis=(2, 4, 6))


def prolong(field):
    extent = field.shape
    spread = jnp.broadcast_to(field[:, :, None, :, None, :, None], (extent[0], extent[1], 2, extent[2], 2, extent[3], 2))
    return spread.reshape(extent[0], extent[1] * 2, extent[2] * 2, extent[3] * 2)


def operator(field, velocity, grads, spacing):
    outputs = []
    for target in range(3):
        component = field[target]
        laplace = -6.0 * component
        advect = jnp.zeros_like(component)
        for across in range(3):
            ahead = jnp.roll(component, -1, across)
            behind = jnp.roll(component, 1, across)
            laplace = laplace + ahead + behind
            advect = advect + velocity[across] * (ahead - behind)
        result_term = (VISCOSITY / (spacing * spacing)) * laplace - advect / (2.0 * spacing)
        for across in range(3):
            result_term = result_term + field[across] * grads[3 * target + across]
        outputs.append(result_term)
    return jnp.stack(outputs)


def reference(velocity, start_field, guess):
    grads = gradients(velocity)
    coarse_vel = restrict(velocity)
    coarse_grads = restrict(grads)
    coarse_init = restrict(start_field)

    def fine(field):
        return operator(field, velocity, grads, 1.0)

    def coarse(field):
        return operator(field, coarse_vel, coarse_grads, 2.0)

    node_values = []
    for slab in range(SLABS):
        begin = start_field if slab == 0 else guess[slab]
        node_values.append([begin, guess[slab], guess[slab]])
    rhs_values = [[fine(field) for field in nodes] for nodes in node_values]
    for sweep_index in range(ITERS):
        if sweep_index > 0:
            for slab in range(SLABS):
                rhs_values[slab][0] = fine(node_values[slab][0])
                rhs_values[slab][2] = fine(node_values[slab][2])
        chained = coarse_init
        for slab in range(SLABS):
            nodes = node_values[slab]
            values = rhs_values[slab]
            integral = TIME_STEP * (values[0] / 6.0 + values[1] * (2.0 / 3.0) + values[2] / 6.0)
            coarse_zero = restrict(nodes[0])
            coarse_end = restrict(nodes[2])
            offset = restrict(integral) - TIME_STEP * coarse(coarse_zero)
            coarse_start = chained
            finish = coarse_start + TIME_STEP * coarse(coarse_start) + offset
            chained = finish
            delta_zero = prolong(coarse_start - coarse_zero)
            delta_end = prolong(finish - coarse_end)
            fixed_zero = nodes[0] + delta_zero
            fixed_mid = nodes[1] + 0.5 * (delta_zero + delta_end)
            fixed_end = nodes[2] + delta_end
            corrected = [fine(fixed_zero), fine(fixed_mid), fine(fixed_end)]
            middle = fixed_zero + TIME_STEP * (corrected[0] * (5.0 / 24.0) + corrected[1] / 3.0 - corrected[2] / 24.0)
            middle_value = fine(middle)
            slab_end = middle + (0.5 * TIME_STEP) * (middle_value - corrected[1]) + TIME_STEP * (-corrected[0] / 24.0 + corrected[1] / 3.0 + corrected[2] * (5.0 / 24.0))
            node_values[slab] = [fixed_zero, middle, slab_end]
            rhs_values[slab] = [corrected[0], middle_value, corrected[2]]
        if sweep_index + 1 < ITERS:
            ends = [node_values[slab][2] for slab in range(SLABS)]
            for slab in range(1, SLABS):
                node_values[slab][0] = ends[slab - 1]
    return jnp.stack([node_values[slab][2] for slab in range(SLABS)])
```

```python
import jax
import jax.numpy as jnp
from jax import lax
from jax.experimental import pallas as pl
from jax.experimental.pallas import tpu as pltpu
from jax.sharding import PartitionSpec as P


MESH = pl.DeviceIdType.MESH
F32 = jnp.float32
NU = 0.125
NUC = 0.03125
FP, CP = 192, 48
NXL, NYL, NZL = 16, 32, 256
NXC = NXL // 2
GUESS, START, NEXT, A1A, A2A, A1B, WRK, YB, VEL = range(9)
NF = 9
CG, CSTART, CNEXT, CV2, CS1, CS2, CE1, CE2, CDX, CDY, CD0 = range(11)
NC = 11
XV, XG, XS, XCG, XCS, XS1, XE1, XA1, XA2, XCV2, XN, XCN, XS2, XE2, XB1 = range(15)
NX_ = 15
TE1, TE2, TZ, TU = range(4)
CHUNKS = 4
NT = TU + CHUNKS


def split3(v):
    hi = v.astype(jnp.bfloat16)
    rest = v - hi.astype(F32)
    mid = rest.astype(jnp.bfloat16)
    low = (rest - mid.astype(F32)).astype(jnp.bfloat16)
    return hi, mid, low


def permute(v, table):
    parts = [jnp.dot(p, table, preferred_element_type=F32) for p in split3(v)]
    return parts[0] + parts[1] + parts[2]


def kernel(vel_hbm, start_hbm, guess_hbm, out_hbm, raw, tmp, fb, gd, fh, fpk, cb, hvc, gc, ch, cpk, off, zin, zout,
           insem, outsem, xss, xrs, tss, trs):
    t, gx, gy = lax.axis_index("tm"), lax.axis_index("gx"), lax.axis_index("gy")
    first = t == 0
    gxm, gxp = lax.rem(gx + 7, 8), lax.rem(gx + 1, 8)
    gym, gyp = lax.rem(gy + 3, 4), lax.rem(gy + 1, 4)
    around = ((gxm, gy), (gxp, gy), (gx, gym), (gx, gyp))
    sub = lax.broadcasted_iota(jnp.int32, (2, 8, 128), 1)
    subc = lax.broadcasted_iota(jnp.int32, (8, 128), 0)
    row_i = lax.broadcasted_iota(jnp.int32, (256, 256), 0)
    col_i = lax.broadcasted_iota(jnp.int32, (256, 256), 1)

    ins = [
        pltpu.make_async_copy(vel_hbm, raw.at[0], insem.at[0]),
        pltpu.make_async_copy(guess_hbm.at[0], raw.at[1], insem.at[1]),
        pltpu.make_async_copy(start_hbm, raw.at[2], insem.at[2]),
    ]
    for copy in ins:
        copy.start()

    bar = pltpu.get_barrier_semaphore()
    for ox, oy in around:
        pl.semaphore_signal(bar, inc=1, device_id=(t, ox, oy), device_id_type=MESH)

    @pl.when(t > 0)
    def _():
        for ox, oy in around + ((gx, gy),):
            pl.semaphore_signal(bar, inc=1, device_id=(t - 1, ox, oy), device_id_type=MESH)

    def exchange(src, dst, pack, halo, which, planes, size, dt=0):
        far = planes * size
        parts = (
            (src.at[pl.ds(size, size)], dst.at[pl.ds(far + size, size)]),
            (src.at[pl.ds(far, size)], dst.at[pl.ds(0, size)]),
            (pack.at[0], halo.at[1]),
            (pack.at[1], halo.at[0]),
        )
        return [
            pltpu.make_async_remote_copy(
                src_ref=s, dst_ref=d, send_sem=xss.at[which, i], recv_sem=xrs.at[which, i],
                device_id=(t + dt, around[i][0], around[i][1]), device_id_type=MESH)
            for i, (s, d) in enumerate(parts)
        ]

    def fine_exchange(k, which):
        return exchange(fb.at[k], fb.at[k], fpk.at[k], fh.at[k], which, NXL, FP)

    def coarse_exchange(k, dst, which, dt=0):
        return exchange(cb.at[k], cb.at[dst], cpk.at[k], ch.at[dst], which, NXC, CP, dt)

    def onward(src, dst, which):
        return pltpu.make_async_remote_copy(
            src_ref=src, dst_ref=dst, send_sem=tss.at[which], recv_sem=trs.at[which],
            device_id=(t + 1, gx, gy), device_id_type=MESH)

    def start(copies, which=(0, 1, 2, 3)):
        for i in which:
            copies[i].start()

    def arrive(copies, which=(0, 1, 2, 3)):
        for i in which:
            copies[i].wait_recv()

    def sent(copies):
        for copy in copies:
            copy.wait_send()

    def fine(k, plane, c, ym):
        return fb[k, pl.ds(pl.multiple_of(plane * FP + (c * 4 + ym) * 16, 16), 16), :].reshape(2, 8, 128)

    def put_fine(k, plane, c, ym, value):
        fb[k, pl.ds(pl.multiple_of(plane * FP + (c * 4 + ym) * 16, 16), 16), :] = value.reshape(16, 128)

    def coarse(k, plane, c, ym):
        return cb[k, pl.ds(pl.multiple_of(plane * CP + (c * 2 + ym) * 8, 8), 8), :]

    def put_coarse(k, plane, c, ym, value):
        cb[k, pl.ds(pl.multiple_of(plane * CP + (c * 2 + ym) * 8, 8), 8), :] = value

    def pack_fine(k):
        for c in range(3):
            for zm in range(2):
                for xm in range(2):
                    at = FP * (1 + xm) + c * 64 + zm * 8
                    to = ((c * 2 + zm) * 2 + xm) * 8
                    fpk[k, 0, pl.ds(to, 8), :] = fb[k, pl.ds(at, 8, stride=2 * FP), :]
                    fpk[k, 1, pl.ds(to, 8), :] = fb[k, pl.ds(at + 48 + 7, 8, stride=2 * FP), :]

    def pack_coarse(k):
        for c in range(3):
            at = CP + c * 16
            cpk[k, 0, pl.ds(c * 8, 8), :] = cb[k, pl.ds(at, 8, stride=CP), :]
            cpk[k, 1, pl.ds(c * 8, 8), :] = cb[k, pl.ds(at + 8 + 7, 8, stride=CP), :]

    def halo_rows(k, side, c, xs, xm):
        rows = [
            jnp.broadcast_to(fh[k, side, pl.ds(((c * 2 + zm) * 2 + xm) * 8 + xs, 1), :], (8, 128)) for zm in range(2)
        ]
        return jnp.stack(rows)

    def halo_row(k, side, c, x):
        return jnp.broadcast_to(ch[k, side, pl.ds(c * 8 + x, 1), :], (8, 128))

    def y_ahead(w, k, c, ym, xs, xm):
        if ym < 3:
            return w[ym + 1]
        return jnp.where(sub == 7, halo_rows(k, 1, c, xs, xm), pltpu.roll(w[0], 7, axis=1))

    def y_behind(w, k, c, ym, xs, xm):
        if ym > 0:
            return w[ym - 1]
        return jnp.where(sub == 0, halo_rows(k, 0, c, xs, xm), pltpu.roll(w[3], 1, axis=1))

    def z_ahead(v):
        return jnp.concatenate([v[1:2], pltpu.roll(v[0:1], 127, axis=2)], axis=0)

    def z_behind(v):
        return jnp.concatenate([pltpu.roll(v[1:2], 1, axis=2), v[0:1]], axis=0)

    def restricted(planes, ym):
        total = planes[0][2 * ym] + planes[0][2 * ym + 1] + planes[1][2 * ym] + planes[1][2 * ym + 1]
        return total[0] + total[1]

    def rhs(k, xs, xm):
        x = 2 * xs + xm
        w = [[fine(k, x + 1, c, ym) for ym in range(4)] for c in range(3)]
        out = [[None] * 4 for _ in range(3)]
        for ym in range(4):
            v = [fine(VEL, x + 1, b, ym) for b in range(3)]
            ahead = [NU - q for q in v]
            behind = [NU + q for q in v]
            for c in range(3):
                total = ahead[0] * fine(k, x + 2, c, ym) + behind[0] * fine(k, x, c, ym)
                total += ahead[1] * y_ahead(w[c], k, c, ym, xs, xm)
                total += behind[1] * y_behind(w[c], k, c, ym, xs, xm)
                total += ahead[2] * z_ahead(w[c][ym])
                total += behind[2] * z_behind(w[c][ym])
                for b in range(3):
                    at = x * (9 * 64) + ((3 * c + b) * 4 + ym) * 16
                    total += w[b][ym] * gd[pl.ds(pl.multiple_of(at, 16), 16), :].reshape(2, 8, 128)
                out[c][ym] = total
        return out

    def coarse_rhs(k, x):
        w = [[coarse(k, x + 1, c, ym) for ym in range(2)] for c in range(3)]
        out = [[None] * 2 for _ in range(3)]
        for ym in range(2):
            v = [hvc[pl.ds(pl.multiple_of(x * CP + (b * 2 + ym) * 8, 8), 8), :] for b in range(3)]
            ahead = [NUC - q for q in v]
            behind = [NUC + q for q in v]
            for c in range(3):
                if ym == 0:
                    ya = w[c][1]
                    yb = jnp.where(subc == 0, halo_row(k, 0, c, x), pltpu.roll(w[c][1], 1, axis=0))
                else:
                    ya = jnp.where(subc == 7, halo_row(k, 1, c, x), pltpu.roll(w[c][0], 7, axis=0))
                    yb = w[c][0]
                total = ahead[0] * coarse(k, x + 2, c, ym) + behind[0] * coarse(k, x, c, ym)
                total += ahead[1] * ya + behind[1] * yb
                total += ahead[2] * pltpu.roll(w[c][ym], 127, axis=1) + behind[2] * pltpu.roll(w[c][ym], 1, axis=1)
                for b in range(3):
                    at = x * 144 + ((3 * c + b) * 2 + ym) * 8
                    total += w[b][ym] * gc[pl.ds(pl.multiple_of(at, 8), 8), :]
                out[c][ym] = total
        return out

    def each(count, body):
        lax.fori_loop(0, count, lambda i, carry: (body(i), carry)[1], 0)

    def crow(x, c, ym):
        return pl.ds(pl.multiple_of(x * CP + (c * 2 + ym) * 8, 8), 8)

    def edges_first(i):
        return jnp.where(i == 0, 0, jnp.where(i == 1, NXC - 1, i - 1))

    def restricted_rhs(k, scale, use):
        def body(xs):
            planes = [rhs(k, xs, xm) for xm in range(2)]
            for c in range(3):
                for ym in range(2):
                    use(xs, c, ym, restricted([p[c] for p in planes], ym) * (scale / 8.0))

        each(NXC, body)

    table = (row_i == 2 * lax.rem(col_i, 128) + col_i // 128).astype(jnp.bfloat16)

    def take(which, k, scale):
        def body(i):
            c, xq = i // 4, lax.rem(i, 4)
            block = raw[which, c, pl.ds(xq * 4, 4)].reshape(128, 256)
            got = permute(block, table)
            if scale != 1.0:
                got = got * scale
            tmp[pl.ds(0, 128), :] = got[:, :128]
            tmp[pl.ds(128, 128), :] = got[:, 128:]
            for xx in range(4):
                for ym in range(4):
                    for zm in range(2):
                        at = (xq * 4 + xx + 1) * FP + c * 64 + (ym * 2 + zm) * 8
                        fb[k, pl.ds(pl.multiple_of(at, 8), 8), :] = tmp[pl.ds(zm * 128 + xx * 32 + ym, 8, stride=4), :]

        each(12, body)

    def means(k, ck):
        def body(xs):
            for c in range(3):
                planes = [[fine(k, 2 * xs + xm + 1, c, ym) for ym in range(4)] for xm in range(2)]
                for ym in range(2):
                    put_coarse(ck, xs + 1, c, ym, restricted(planes, ym) * 0.125)

        each(NXC, body)

    xv = fine_exchange(VEL, XV)
    xg = fine_exchange(GUESS, XG)
    xs_ = fine_exchange(START, XS)
    xcg = coarse_exchange(CG, CG, XCG)
    xcs = coarse_exchange(CSTART, CSTART, XCS)

    ins[0].wait()
    take(0, VEL, 0.25)
    pack_fine(VEL)

    @pl.when(t < 3)
    def _():
        pl.semaphore_wait(bar, 9)

    @pl.when(t == 3)
    def _():
        pl.semaphore_wait(bar, 4)

    start(xv)
    ins[1].wait()
    take(1, GUESS, 1.0)
    pack_fine(GUESS)
    start(xg)
    means(GUESS, CG)
    pack_coarse(CG)
    start(xcg)
    ins[2].wait()

    @pl.when(first)
    def _():
        take(2, START, 1.0)
        pack_fine(START)
        start(xs_)
        means(START, CSTART)
        pack_coarse(CSTART)
        start(xcs)

    arrive(xv)

    def gradients(xs):
        for a in range(3):
            kept = [[None, None] for _ in range(3)]
            vel = [None, None]
            for xm in range(2):
                x = 2 * xs + xm
                w = [fine(VEL, x + 1, a, ym) for ym in range(4)]
                vel[xm] = w
                diffs = [[None] * 4 for _ in range(3)]
                for ym in range(4):
                    diffs[0][ym] = fine(VEL, x + 2, a, ym) - fine(VEL, x, a, ym)
                    diffs[1][ym] = y_ahead(w, VEL, a, ym, xs, xm) - y_behind(w, VEL, a, ym, xs, xm)
                    diffs[2][ym] = z_ahead(w[ym]) - z_behind(w[ym])
                for b in range(3):
                    for ym in range(4):
                        if a == b:
                            diffs[b][ym] = diffs[b][ym] - 6.0 * NU
                        at = x * (9 * 64) + ((3 * a + b) * 4 + ym) * 16
                        gd[pl.ds(pl.multiple_of(at, 16), 16), :] = diffs[b][ym].reshape(16, 128)
                    kept[b][xm] = diffs[b]
            for ym in range(2):
                hvc[crow(xs, a, ym), :] = restricted(vel, ym) * 0.0625
                for b in range(3):
                    at = xs * 144 + ((3 * a + b) * 2 + ym) * 8
                    mean = restricted(kept[b], ym) * 0.125
                    if a == b:
                        mean = mean + 6.0 * (NU - NUC)
                    gc[pl.ds(pl.multiple_of(at, 8), 8), :] = mean

    each(NXC, gradients)
    arrive(xg)
    arrive(xcg)

    @pl.when(first)
    def _():
        arrive(xs_)
        arrive(xcs)

        def combine(i):
            for j in range(12):
                at = pl.ds(pl.multiple_of(i * FP + j * 16, 16), 16)
                fb[WRK, at, :] = fb[START, at, :] * (1.0 / 6.0) + fb[GUESS, at, :] * (5.0 / 6.0)

        each(NXL + 2, combine)
        for side in range(2):
            fh[WRK, side] = fh[START, side] * (1.0 / 6.0) + fh[GUESS, side] * (5.0 / 6.0)

    def keep_offset(x, c, ym, value):
        off[crow(x, c, ym), :] = value

    restricted_rhs(jnp.where(first, WRK, GUESS), 1.0, keep_offset)

    u0_1 = jnp.where(first, START, GUESS)
    u0_2 = jnp.where(first, START, NEXT)
    v0_1 = jnp.where(first, CSTART, CG)
    v0_2 = jnp.where(first, CSTART, CNEXT)
    s_1 = jnp.where(first, CSTART, CS1)
    s_2 = jnp.where(first, CSTART, CS2)

    def less_start(x):
        out = coarse_rhs(v0_1, x)
        for c in range(3):
            for ym in range(2):
                at = crow(x, c, ym)
                off[at, :] = off[at, :] - out[c][ym]

    each(NXC, less_start)

    inner = pl.ds(CP, NXC * CP)

    def chain(ks, ke, xs_id, xe_id, te):
        to_next = onward(cb.at[ke, inner], cb.at[{CE1: CS1, CE2: CS2}[ke], inner], te)
        skew = coarse_exchange(ke, {CE1: CS1, CE2: CS2}[ke], xs_id, 1)
        same = coarse_exchange(ke, ke, xe_id)

        @pl.when(t > 0)
        def _():
            arrive(skew)
            to_next.wait_recv()

        def body(x):
            out = coarse_rhs(ks, x)
            for c in range(3):
                for ym in range(2):
                    put_coarse(ke, x + 1, c, ym, coarse(ks, x + 1, c, ym) + out[c][ym] + off[crow(x, c, ym), :])

        each(NXC, body)
        pack_coarse(ke)

        @pl.when(t < 3)
        def _():
            start(skew)
            to_next.start()

        start(same)
        return to_next, skew, same

    next1, skew1, same1 = chain(s_1, CE1, XS1, XE1, TE1)

    @pl.when(first)
    def _():
        def keep(x, c, ym, value):
            zin[crow(x, c, ym), :] = value

        restricted_rhs(START, 1.0 / 6.0, keep)

        def less(x):
            out = coarse_rhs(CSTART, x)
            for c in range(3):
                for ym in range(2):
                    at = crow(x, c, ym)
                    zin[at, :] = zin[at, :] - out[c][ym]

        each(NXC, less)

    def sweep(ku0, kv0, ks, kv2, ke, k1, k2, ka1, ka2, xa_id, after_edges, mean_of):
        def corrections(x):
            for c in range(3):
                for ym in range(2):
                    d0 = coarse(ks, x, c, ym) - coarse(kv0, x, c, ym)
                    d2 = coarse(ke, x, c, ym) - coarse(kv2, x, c, ym)
                    put_coarse(CD0, x, c, ym, d0)
                    put_coarse(CDX, x, c, ym, 0.375 * d0 + 0.125 * d2)
                    put_coarse(CDY, x, c, ym, 0.125 * (d2 - d0))

        each(NXC + 2, corrections)
        for side in range(2):
            d0 = ch[ks, side] - ch[kv0, side]
            d2 = ch[ke, side] - ch[kv2, side]
            ch[CDX, side] = 0.375 * d0 + 0.125 * d2
            ch[CDY, side] = 0.125 * (d2 - d0)

        def x_of(u0, u1, u2, d):
            if k1 == k2:
                return (5.0 / 24.0) * u0 + (7.0 / 24.0) * u1 + d
            return (5.0 / 24.0) * u0 + (1.0 / 3.0) * u1 - (1.0 / 24.0) * u2 + d

        def y_of(a1, u0, u1, u2, d):
            if k1 == k2:
                return 0.5 * a1 - (1.0 / 24.0) * u0 + (1.0 / 24.0) * u1 + d
            return 0.5 * a1 - (1.0 / 24.0) * u0 - (1.0 / 6.0) * u1 + (5.0 / 24.0) * u2 + d

        def x_plane(p):
            xc = (p + 1) // 2
            for c in range(3):
                for ym in range(4):
                    d = coarse(CDX, xc, c, ym // 2)[None]
                    put_fine(WRK, p, c, ym, x_of(fine(ku0, p, c, ym), fine(k1, p, c, ym), fine(k2, p, c, ym), d))

        each(NXL + 2, x_plane)

        def halo_blocks():
            for side in range(2):
                for c in range(3):
                    for j in range(4):
                        yield side, c, pl.ds((c * 4 + j) * 8, 8)

        for side, c, at in halo_blocks():
            d = ch[CDX, side, pl.ds(c * 8, 8), :]
            fh[WRK, side, at, :] = x_of(fh[ku0, side, at, :], fh[k1, side, at, :], fh[k2, side, at, :], d)

        xa = fine_exchange(ka1, xa_id)

        def first_node(i):
            xs = edges_first(i)
            for xm in range(2):
                out = rhs(WRK, xs, xm)
                p = 2 * xs + xm + 1
                for c in range(3):
                    for ym in range(4):
                        u0 = fine(ku0, p, c, ym)
                        a1 = u0 + coarse(CD0, xs + 1, c, ym // 2)[None] + out[c][ym]
                        put_fine(ka1, p, c, ym, a1)
                        d = coarse(CDY, xs + 1, c, ym // 2)[None]
                        put_fine(YB, p, c, ym, y_of(a1, u0, fine(k1, p, c, ym), fine(k2, p, c, ym), d))

            @pl.when(i == 1)
            def _():
                start(xa, (0, 1))

        each(NXC, first_node)
        pack_fine(ka1)
        start(xa, (2, 3))

        def y_halo_plane(p, xc):
            for c in range(3):
                for ym in range(4):
                    d = coarse(CDY, xc, c, ym // 2)[None]
                    put_fine(YB, p, c, ym, y_of(fine(ka1, p, c, ym), fine(ku0, p, c, ym), fine(k1, p, c, ym), fine(k2, p, c, ym), d))

        arrive(xa, (0, 1))
        y_halo_plane(0, 0)
        y_halo_plane(NXL + 1, NXC + 1)
        arrive(xa, (2, 3))
        for side, c, at in halo_blocks():
            d = ch[CDY, side, pl.ds(c * 8, 8), :]
            fh[YB, side, at, :] = y_of(fh[ka1, side, at, :], fh[ku0, side, at, :], fh[k1, side, at, :], fh[k2, side, at, :], d)

        def second_node(i):
            xs = edges_first(i)
            planes = []
            for xm in range(2):
                out = rhs(YB, xs, xm)
                p = 2 * xs + xm + 1
                for c in range(3):
                    for ym in range(4):
                        out[c][ym] = fine(ka1, p, c, ym) + out[c][ym]
                        put_fine(ka2, p, c, ym, out[c][ym])
                planes.append(out)
            if mean_of is not None:
                for c in range(3):
                    for ym in range(2):
                        put_coarse(mean_of, xs + 1, c, ym, restricted([q[c] for q in planes], ym) * 0.125)
            if after_edges is not None:
                @pl.when(i == 1)
                def _():
                    after_edges()

        each(NXC, second_node)
        return xa

    arrive(same1)
    xa2 = fine_exchange(A2A, XA2)
    xcv2 = coarse_exchange(CV2, CV2, XCV2)

    def send_edges():
        start(xa2, (0, 1))
        start(xcv2, (0, 1))

    xa1 = sweep(u0_1, v0_1, s_1, CG, CE1, GUESS, GUESS, A1A, A2A, XA1, send_edges, CV2)
    pack_fine(A2A)
    start(xa2, (2, 3))
    pack_coarse(CV2)
    start(xcv2, (2, 3))

    rows = NXL * FP // CHUNKS
    bulk = [
        onward(fb.at[A2A, pl.ds(FP + i * rows, rows)], fb.at[NEXT, pl.ds(FP + i * rows, rows)], TU + i)
        for i in range(CHUNKS)
    ]
    to_z = onward(zout, zin, TZ)

    def send_bulk(which):
        @pl.when(t < 3)
        def _():
            for i in which:
                bulk[i].start()

    send_bulk((0, 1))
    restricted_rhs(A1A, 2.0 / 3.0, keep_offset)
    arrive(xa2)
    arrive(xcv2)

    def both(x, c, ym, value):
        at = crow(x, c, ym)
        off[at, :] = off[at, :] + value
        zout[at, :] = value

    restricted_rhs(A2A, 1.0 / 6.0, both)

    def less_end(x):
        out = coarse_rhs(CV2, x)
        for c in range(3):
            for ym in range(2):
                at = crow(x, c, ym)
                zout[at, :] = zout[at, :] - out[c][ym]

    each(NXC, less_end)

    @pl.when(t < 3)
    def _():
        to_z.start()

    @pl.when(t > 0)
    def _():
        to_z.wait_recv()

    def add_previous(x):
        for c in range(3):
            for ym in range(2):
                at = crow(x, c, ym)
                off[at, :] = off[at, :] + zin[at, :]

    each(NXC, add_previous)
    next2, skew2, same2 = chain(s_2, CE2, XS2, XE2, TE2)
    send_bulk(tuple(range(2, CHUNKS)))

    xn = fine_exchange(NEXT, XN)
    xcn = coarse_exchange(CNEXT, CNEXT, XCN)

    @pl.when(t > 0)
    def _():
        for copy in bulk:
            copy.wait_recv()
        start(xn, (0, 1))
        pack_fine(NEXT)
        start(xn, (2, 3))
        means(NEXT, CNEXT)
        pack_coarse(CNEXT)
        start(xcn)
        arrive(xn)
        arrive(xcn)

    arrive(same2)
    xb1 = sweep(u0_2, v0_2, s_2, CV2, CE2, A1A, A2A, A1B, WRK, XB1, None, None)

    back = (col_i == 2 * lax.rem(row_i, 128) + row_i // 128).astype(jnp.bfloat16)

    def give(i):
        c, xq = i // 4, lax.rem(i, 4)
        for xx in range(4):
            for ym in range(4):
                for zm in range(2):
                    at = (xq * 4 + xx + 1) * FP + c * 64 + (ym * 2 + zm) * 8
                    tmp[pl.ds(zm * 128 + xx * 32 + ym, 8, stride=4), :] = fb[WRK, pl.ds(pl.multiple_of(at, 8), 8), :]
        block = jnp.concatenate([tmp[pl.ds(0, 128), :], tmp[pl.ds(128, 128), :]], axis=1)
        raw[0, c, pl.ds(xq * 4, 4)] = permute(block, back).reshape(4, 32, 256)

    each(12, give)
    out = pltpu.make_async_copy(raw.at[0], out_hbm.at[0], outsem)
    out.start()

    for copies in (xv, xg, xcg, same1, xa1, xa2, xcv2, same2, xb1):
        sent(copies)

    @pl.when(first)
    def _():
        sent(xs_)
        sent(xcs)

    @pl.when(t > 0)
    def _():
        sent(xn)
        sent(xcn)

    @pl.when(t < 3)
    def _():
        for copies in (skew1, skew2, [next1, next2, to_z], bulk):
            sent(copies)

    out.wait()


def shards(velocity, start_field, guess):
    anywhere = pl.BlockSpec(memory_space=pl.ANY)
    return pl.pallas_call(
        kernel,
        out_shape=jax.ShapeDtypeStruct((1, 3, NXL, NYL, NZL), F32),
        in_specs=[anywhere] * 3,
        out_specs=anywhere,
        scratch_shapes=[
            pltpu.VMEM((3, 3, NXL, NYL, NZL), F32),
            pltpu.VMEM((256, 128), F32),
            pltpu.VMEM((NF, (NXL + 2) * FP, 128), F32),
            pltpu.VMEM((NXL * 9 * 64, 128), F32),
            pltpu.VMEM((NF, 2, 96, 128), F32),
            pltpu.VMEM((NF, 2, 96, 128), F32),
            pltpu.VMEM((NC, (NXC + 2) * CP, 128), F32),
            pltpu.VMEM((NXC * CP, 128), F32),
            pltpu.VMEM((NXC * 144, 128), F32),
            pltpu.VMEM((NC, 2, 24, 128), F32),
            pltpu.VMEM((NC, 2, 24, 128), F32),
            pltpu.VMEM((NXC * CP, 128), F32),
            pltpu.VMEM((NXC * CP, 128), F32),
            pltpu.VMEM((NXC * CP, 128), F32),
            pltpu.SemaphoreType.DMA((3,)),
            pltpu.SemaphoreType.DMA,
            pltpu.SemaphoreType.DMA((NX_, 4)),
            pltpu.SemaphoreType.DMA((NX_, 4)),
            pltpu.SemaphoreType.DMA((NT,)),
            pltpu.SemaphoreType.DMA((NT,)),
        ],
        compiler_params=pltpu.CompilerParams(
            collective_id=0, has_side_effects=True, vmem_limit_bytes=60 * 1024 * 1024
        ),
        name="pfasst",
    )(velocity, start_field, guess)


def solution(mesh):
    in_specs = (
        P(None, "gx", "gy", None),
        P(None, "gx", "gy", None),
        P("tm", None, "gx", "gy", None),
    )
    out_specs = P("tm", None, "gx", "gy", None)
    return jax.shard_map(shards, mesh=mesh, in_specs=in_specs, out_specs=out_specs, check_vma=False)
```

```python
import jax
import jax.numpy as jnp
from jax import lax
from jax.experimental import pallas as pl
from jax.experimental.pallas import tpu as pltpu
from jax.sharding import PartitionSpec as P


MESH = pl.DeviceIdType.MESH
F32 = jnp.float32
NU = 0.125
NUC = 0.03125
FP, CP = 192, 48
NXL, NYL, NZL = 16, 32, 256
NXC = NXL // 2
GUESS, START, NEXT, A1A, A2A, A1B, WRK, YB, VEL, A1P, WRKP, YBP = range(12)
NF = 12
CG, CSTART, CNEXT, CV2, CS1, CS2, CE1, CE2, CPS, CDX, CDY, CD0, CDXP, CDYP, CD0P = range(15)
NC = 15
XV, XG, XS, XCG, XCS, XS1, XE1, XA1, XA2, XCV2, XN, XCN, XS2, XE2, XB1, XW, XAP = range(17)
NX_ = 17
TE1, TE2, TZ, TU, TP, TPH, TG = range(7)
NT = TG + 3
PLANES = 4


def split3(v):
    hi = v.astype(jnp.bfloat16)
    rest = v - hi.astype(F32)
    mid = rest.astype(jnp.bfloat16)
    low = (rest - mid.astype(F32)).astype(jnp.bfloat16)
    return hi, mid, low


def permute(v, table):
    parts = [jnp.dot(p, table, preferred_element_type=F32) for p in split3(v)]
    return parts[0] + parts[1] + parts[2]


def kernel(vel_hbm, start_hbm, guess_hbm, out_hbm, raw, fb, gd, fh, fpk, cb, hvc, gc, ch, cpk, off, zin, zout,
           insem, outsem, xss, xrs, tss, trs):
    t, gx, gy = lax.axis_index("tm"), lax.axis_index("gx"), lax.axis_index("gy")
    first = t == 0
    gxm, gxp = lax.rem(gx + 7, 8), lax.rem(gx + 1, 8)
    gym, gyp = lax.rem(gy + 3, 4), lax.rem(gy + 1, 4)
    around = ((gxm, gy), (gxp, gy), (gx, gym), (gx, gyp))
    sub = lax.broadcasted_iota(jnp.int32, (2, 8, 128), 1)
    subc = lax.broadcasted_iota(jnp.int32, (8, 128), 0)
    row_i = lax.broadcasted_iota(jnp.int32, (256, 256), 0)
    col_i = lax.broadcasted_iota(jnp.int32, (256, 256), 1)

    def load(hbm, which):
        return [
            pltpu.make_async_copy(hbm.at[:, :, :, pl.ds(h * 128, 128)], raw.at[which, :, h], insem.at[which, h])
            for h in range(2)
        ]

    ins = [load(vel_hbm, 0), load(guess_hbm.at[0], 1), load(start_hbm, 2)]
    for copy in ins[0] + ins[1]:
        copy.start()

    @pl.when(first)
    def _():
        for copy in ins[2]:
            copy.start()

    bar = pltpu.get_barrier_semaphore()
    for ox, oy in around:
        pl.semaphore_signal(bar, inc=1, device_id=(t, ox, oy), device_id_type=MESH)

    @pl.when(t > 0)
    def _():
        pl.semaphore_signal(bar, inc=1, device_id=(t - 1, gx, gy), device_id_type=MESH)

    def exchange(src, dst, pack, halo, which, planes, size, dt=0):
        far = planes * size
        parts = (
            (src.at[pl.ds(size, size)], dst.at[pl.ds(far + size, size)]),
            (src.at[pl.ds(far, size)], dst.at[pl.ds(0, size)]),
            (pack.at[0], halo.at[1]),
            (pack.at[1], halo.at[0]),
        )
        return [
            pltpu.make_async_remote_copy(
                src_ref=s, dst_ref=d, send_sem=xss.at[which, i], recv_sem=xrs.at[which, i],
                device_id=(t + dt, around[i][0], around[i][1]), device_id_type=MESH)
            for i, (s, d) in enumerate(parts)
        ]

    def fine_exchange(k, which):
        return exchange(fb.at[k], fb.at[k], fpk.at[k], fh.at[k], which, NXL, FP)

    def coarse_exchange(k, dst, which, dt=0):
        return exchange(cb.at[k], cb.at[dst], cpk.at[k], ch.at[dst], which, NXC, CP, dt)

    def onward(src, dst, which):
        return pltpu.make_async_remote_copy(
            src_ref=src, dst_ref=dst, send_sem=tss.at[which], recv_sem=trs.at[which],
            device_id=(t + 1, gx, gy), device_id_type=MESH)

    def start(copies, which=(0, 1, 2, 3)):
        for i in which:
            copies[i].start()

    def arrive(copies, which=(0, 1, 2, 3)):
        for i in which:
            copies[i].wait_recv()

    def sent(copies):
        for copy in copies:
            copy.wait_send()

    def fine(k, plane, c, ym):
        return fb[k, pl.ds(pl.multiple_of(plane * FP + (c * 4 + ym) * 16, 16), 16), :].reshape(2, 8, 128)

    def put_fine(k, plane, c, ym, value):
        fb[k, pl.ds(pl.multiple_of(plane * FP + (c * 4 + ym) * 16, 16), 16), :] = value.reshape(16, 128)

    def coarse(k, plane, c, ym):
        return cb[k, pl.ds(pl.multiple_of(plane * CP + (c * 2 + ym) * 8, 8), 8), :]

    def put_coarse(k, plane, c, ym, value):
        cb[k, pl.ds(pl.multiple_of(plane * CP + (c * 2 + ym) * 8, 8), 8), :] = value

    def pack_fine(k):
        for c in range(3):
            for zm in range(2):
                for xm in range(2):
                    at = FP * (1 + xm) + c * 64 + zm * 8
                    to = ((c * 2 + zm) * 2 + xm) * 8
                    fpk[k, 0, pl.ds(to, 8), :] = fb[k, pl.ds(at, 8, stride=2 * FP), :]
                    fpk[k, 1, pl.ds(to, 8), :] = fb[k, pl.ds(at + 48 + 7, 8, stride=2 * FP), :]

    def pack_coarse(k):
        for c in range(3):
            at = CP + c * 16
            cpk[k, 0, pl.ds(c * 8, 8), :] = cb[k, pl.ds(at, 8, stride=CP), :]
            cpk[k, 1, pl.ds(c * 8, 8), :] = cb[k, pl.ds(at + 8 + 7, 8, stride=CP), :]

    def halo_rows(k, side, c, xs, xm):
        rows = [
            jnp.broadcast_to(fh[k, side, pl.ds(((c * 2 + zm) * 2 + xm) * 8 + xs, 1), :], (8, 128)) for zm in range(2)
        ]
        return jnp.stack(rows)

    def halo_row(k, side, c, x):
        return jnp.broadcast_to(ch[k, side, pl.ds(c * 8 + x, 1), :], (8, 128))

    def y_ahead(w, k, c, ym, xs, xm):
        if ym < 3:
            return w[ym + 1]
        return jnp.where(sub == 7, halo_rows(k, 1, c, xs, xm), pltpu.roll(w[0], 7, axis=1))

    def y_behind(w, k, c, ym, xs, xm):
        if ym > 0:
            return w[ym - 1]
        return jnp.where(sub == 0, halo_rows(k, 0, c, xs, xm), pltpu.roll(w[3], 1, axis=1))

    def z_ahead(v):
        return jnp.concatenate([v[1:2], pltpu.roll(v[0:1], 127, axis=2)], axis=0)

    def z_behind(v):
        return jnp.concatenate([pltpu.roll(v[1:2], 1, axis=2), v[0:1]], axis=0)

    def restricted(planes, ym):
        total = planes[0][2 * ym] + planes[0][2 * ym + 1] + planes[1][2 * ym] + planes[1][2 * ym + 1]
        return total[0] + total[1]

    def rhs(k, xs, xm):
        x = 2 * xs + xm
        w = [[fine(k, x + 1, c, ym) for ym in range(4)] for c in range(3)]
        out = [[None] * 4 for _ in range(3)]
        for ym in range(4):
            v = [fine(VEL, x + 1, b, ym) for b in range(3)]
            ahead = [NU - q for q in v]
            behind = [NU + q for q in v]
            for c in range(3):
                total = ahead[0] * fine(k, x + 2, c, ym) + behind[0] * fine(k, x, c, ym)
                total += ahead[1] * y_ahead(w[c], k, c, ym, xs, xm)
                total += behind[1] * y_behind(w[c], k, c, ym, xs, xm)
                total += ahead[2] * z_ahead(w[c][ym])
                total += behind[2] * z_behind(w[c][ym])
                for b in range(3):
                    at = x * (9 * 64) + ((3 * c + b) * 4 + ym) * 16
                    total += w[b][ym] * gd[pl.ds(pl.multiple_of(at, 16), 16), :].reshape(2, 8, 128)
                out[c][ym] = total
        return out

    def coarse_rhs(k, x):
        w = [[coarse(k, x + 1, c, ym) for ym in range(2)] for c in range(3)]
        out = [[None] * 2 for _ in range(3)]
        for ym in range(2):
            v = [hvc[pl.ds(pl.multiple_of(x * CP + (b * 2 + ym) * 8, 8), 8), :] for b in range(3)]
            ahead = [NUC - q for q in v]
            behind = [NUC + q for q in v]
            for c in range(3):
                if ym == 0:
                    ya = w[c][1]
                    yb = jnp.where(subc == 0, halo_row(k, 0, c, x), pltpu.roll(w[c][1], 1, axis=0))
                else:
                    ya = jnp.where(subc == 7, halo_row(k, 1, c, x), pltpu.roll(w[c][0], 7, axis=0))
                    yb = w[c][0]
                total = ahead[0] * coarse(k, x + 2, c, ym) + behind[0] * coarse(k, x, c, ym)
                total += ahead[1] * ya + behind[1] * yb
                total += ahead[2] * pltpu.roll(w[c][ym], 127, axis=1) + behind[2] * pltpu.roll(w[c][ym], 1, axis=1)
                for b in range(3):
                    at = x * 144 + ((3 * c + b) * 2 + ym) * 8
                    total += w[b][ym] * gc[pl.ds(pl.multiple_of(at, 8), 8), :]
                out[c][ym] = total
        return out

    def each(count, body, unroll=1):
        lax.fori_loop(0, count, lambda i, carry: (body(i), carry)[1], 0, unroll=unroll)

    def crow(x, c, ym):
        return pl.ds(pl.multiple_of(x * CP + (c * 2 + ym) * 8, 8), 8)

    def edges_first(i):
        return jnp.where(i == 0, 0, jnp.where(i == 1, NXC - 1, i - 1))

    def restricted_rhs(k, scale, use):
        def body(xs):
            planes = [rhs(k, xs, xm) for xm in range(2)]
            for c in range(3):
                for ym in range(2):
                    use(xs, c, ym, restricted([p[c] for p in planes], ym) * (scale / 8.0))

        each(NXC, body)

    table = (row_i == 2 * lax.rem(col_i, 128) + col_i // 128).astype(jnp.bfloat16)

    def take(read, k, c_from=0, c_to=3):
        def body(i):
            c, xq = i // 4, lax.rem(i, 4)
            got = permute(read(c, xq), table)
            for xx in range(4):
                for ym in range(4):
                    for zm in range(2):
                        at = (xq * 4 + xx + 1) * FP + c * 64 + (ym * 2 + zm) * 8
                        row = (xx * 4 + ym) * 8
                        fb[k, pl.ds(pl.multiple_of(at, 8), 8), :] = got[row : row + 8, zm * 128 : (zm + 1) * 128]

        lax.fori_loop(4 * c_from, 4 * c_to, lambda i, carry: (body(i), carry)[1], 0, unroll=2)

    def raw_rows(which):
        def read(c, xq):
            blocks = []
            for xx in range(4):
                for ym in range(4):
                    rows = [raw[which, c, h, xq * 4 + xx, pl.ds(ym, 8, stride=4), :] for h in range(2)]
                    blocks.append(jnp.concatenate(rows, axis=1))
            return jnp.concatenate(blocks, axis=0)

        return read

    def means(k, ck):
        def body(xs):
            for c in range(3):
                planes = [[fine(k, 2 * xs + xm + 1, c, ym) for ym in range(4)] for xm in range(2)]
                for ym in range(2):
                    put_coarse(ck, xs + 1, c, ym, restricted(planes, ym) * 0.125)

        each(NXC, body, 2)

    xv = fine_exchange(VEL, XV)
    xw = fine_exchange(WRK, XW)
    xg = fine_exchange(GUESS, XG)
    xs_ = fine_exchange(START, XS)
    xcg = coarse_exchange(CG, CG, XCG)

    for copy in ins[0]:
        copy.wait()
    take(lambda c, xq: raw_rows(0)(c, xq) * 0.25, VEL)
    pack_fine(VEL)

    @pl.when(t < 3)
    def _():
        pl.semaphore_wait(bar, 5)

    @pl.when(t == 3)
    def _():
        pl.semaphore_wait(bar, 4)

    start(xv)
    for copy in ins[1]:
        copy.wait()
    guess_on = [onward(raw.at[1, c], raw.at[2, c], TG + c) for c in range(3)]

    @pl.when(t == 1)
    def _():
        guess_on[0].start()

    @pl.when(first)
    def _():
        for copy in ins[2]:
            copy.wait()
        take(lambda c, xq: raw_rows(2)(c, xq) * (1.0 / 6.0) + raw_rows(1)(c, xq) * (5.0 / 6.0), WRK)
        pack_fine(WRK)
        start(xw)

    take(raw_rows(1), GUESS)
    pack_fine(GUESS)
    start(xg)
    means(GUESS, CG)
    pack_coarse(CG)
    start(xcg)

    @pl.when(t == 1)
    def _():
        guess_on[1].start()

    @pl.when(first)
    def _():
        take(raw_rows(2), START)
        pack_fine(START)
        start(xs_)
        means(START, CSTART)
        for side in range(2):
            ch[CSTART, side] = jnp.zeros((24, 128), F32)
            cb[CSTART, pl.ds(side * (NXC + 1) * CP, CP), :] = jnp.zeros((CP, 128), F32)

    arrive(xv)

    def gradients(xs):
        for a in range(3):
            kept = [[None, None] for _ in range(3)]
            vel = [None, None]
            for xm in range(2):
                x = 2 * xs + xm
                w = [fine(VEL, x + 1, a, ym) for ym in range(4)]
                vel[xm] = w
                diffs = [[None] * 4 for _ in range(3)]
                for ym in range(4):
                    diffs[0][ym] = fine(VEL, x + 2, a, ym) - fine(VEL, x, a, ym)
                    diffs[1][ym] = y_ahead(w, VEL, a, ym, xs, xm) - y_behind(w, VEL, a, ym, xs, xm)
                    diffs[2][ym] = z_ahead(w[ym]) - z_behind(w[ym])
                for b in range(3):
                    for ym in range(4):
                        if a == b:
                            diffs[b][ym] = diffs[b][ym] - 6.0 * NU
                        at = x * (9 * 64) + ((3 * a + b) * 4 + ym) * 16
                        gd[pl.ds(pl.multiple_of(at, 16), 16), :] = diffs[b][ym].reshape(16, 128)
                    kept[b][xm] = diffs[b]
            for ym in range(2):
                hvc[crow(xs, a, ym), :] = restricted(vel, ym) * 0.0625
                for b in range(3):
                    at = xs * 144 + ((3 * a + b) * 2 + ym) * 8
                    mean = restricted(kept[b], ym) * 0.125
                    if a == b:
                        mean = mean + 6.0 * (NU - NUC)
                    gc[pl.ds(pl.multiple_of(at, 8), 8), :] = mean

    each(NXC, gradients)

    @pl.when(first)
    def _():
        arrive(xw)

    @pl.when(t > 0)
    def _():
        arrive(xg)
        arrive(xcg)

    def keep_offset(x, c, ym, value):
        off[crow(x, c, ym), :] = value

    restricted_rhs(jnp.where(first, WRK, GUESS), 1.0, keep_offset)

    u0_1 = jnp.where(first, START, GUESS)
    u0_2 = jnp.where(first, START, NEXT)
    v0_1 = jnp.where(first, CSTART, CG)
    v0_2 = jnp.where(first, CSTART, CNEXT)
    s_1 = jnp.where(first, CSTART, CS1)
    s_2 = jnp.where(first, CSTART, CS2)

    @pl.when(t > 0)
    def _():
        def less_start(x):
            out = coarse_rhs(CG, x)
            for c in range(3):
                for ym in range(2):
                    at = crow(x, c, ym)
                    off[at, :] = off[at, :] - out[c][ym]

        each(NXC, less_start, 4)

    inner = pl.ds(CP, NXC * CP)

    def chain(ks, ke, xs_id, xe_id, te):
        to_next = onward(cb.at[ke, inner], cb.at[{CE1: CS1, CE2: CS2}[ke], inner], te)
        skew = coarse_exchange(ke, {CE1: CS1, CE2: CS2}[ke], xs_id, 1)
        same = coarse_exchange(ke, ke, xe_id)

        @pl.when(t > 0)
        def _():
            arrive(skew)
            to_next.wait_recv()

            def body(x):
                out = coarse_rhs(ks, x)
                for c in range(3):
                    for ym in range(2):
                        put_coarse(ke, x + 1, c, ym, coarse(ks, x + 1, c, ym) + out[c][ym] + off[crow(x, c, ym), :])

            each(NXC, body, 4)

        @pl.when(first)
        def _():
            def body(x):
                for c in range(3):
                    for ym in range(2):
                        put_coarse(ke, x + 1, c, ym, coarse(CSTART, x + 1, c, ym) + off[crow(x, c, ym), :])

            each(NXC, body, 4)

        pack_coarse(ke)

        @pl.when(t < 3)
        def _():
            start(skew)
            to_next.start()

        start(same)
        return to_next, skew, same

    xcs = coarse_exchange(CSTART, CSTART, XCS)

    @pl.when(t == 2)
    def _():
        for c in range(2):
            guess_on[c].wait_recv()
            take(raw_rows(2), START, c, c + 1)

    next1, skew1, same1 = chain(CS1, CE1, XS1, XE1, TE1)

    before_on = [onward(cb.at[CS1], cb.at[CPS], TP), onward(ch.at[CS1], ch.at[CPS], TPH)]

    @pl.when(t == 1)
    def _():
        for copy in before_on + [guess_on[2]]:
            copy.start()

    @pl.when(first)
    def _():
        arrive(xs_)
        arrive(xg)
        arrive(xcg)
        sent(xw)

        def keep(x, c, ym, value):
            zin[crow(x, c, ym), :] = value

        restricted_rhs(START, 1.0 / 6.0, keep)

    def give(xs):
        at = pl.ds(pl.multiple_of(xs * 2 * FP, 2 * FP), 2 * FP)
        return pltpu.make_async_copy(fb.at[WRK, pl.ds(pl.multiple_of(xs * 2 * FP + FP, FP), 2 * FP)], out_hbm.at[at], outsem.at[xs])

    def sweep(ku0, kv0, ks, kv2, ke, k1, k2, ka1, ka2, xa_id, after_edges, mean_of, kx=WRK, ky=YB, kdx=CDX, kdy=CDY, kd0=CD0):
        def corrections(x):
            for c in range(3):
                for ym in range(2):
                    d0 = coarse(ks, x, c, ym) - coarse(kv0, x, c, ym)
                    d2 = coarse(ke, x, c, ym) - coarse(kv2, x, c, ym)
                    put_coarse(kd0, x, c, ym, d0)
                    put_coarse(kdx, x, c, ym, 0.375 * d0 + 0.125 * d2)
                    put_coarse(kdy, x, c, ym, 0.125 * (d2 - d0))

        def x_of(u0, u1, u2, d):
            if k1 == k2:
                return (5.0 / 24.0) * u0 + (7.0 / 24.0) * u1 + d
            return (5.0 / 24.0) * u0 + (1.0 / 3.0) * u1 - (1.0 / 24.0) * u2 + d

        def y_of(a1, u0, u1, u2, d):
            if k1 == k2:
                return 0.5 * a1 - (1.0 / 24.0) * u0 + (1.0 / 24.0) * u1 + d
            return 0.5 * a1 - (1.0 / 24.0) * u0 - (1.0 / 6.0) * u1 + (5.0 / 24.0) * u2 + d

        def x_plane(p):
            xc = (p + 1) // 2
            for c in range(3):
                for ym in range(4):
                    d = coarse(kdx, xc, c, ym // 2)[None]
                    put_fine(kx, p, c, ym, x_of(fine(ku0, p, c, ym), fine(k1, p, c, ym), fine(k2, p, c, ym), d))

        def halo_blocks():
            for side in range(2):
                for c in range(3):
                    for j in range(4):
                        yield side, c, pl.ds((c * 4 + j) * 8, 8)

        xa = fine_exchange(ka1, xa_id)

        def first_node(i):
            xs = edges_first(i)
            for xm in range(2):
                out = rhs(kx, xs, xm)
                p = 2 * xs + xm + 1
                for c in range(3):
                    for ym in range(4):
                        u0 = fine(ku0, p, c, ym)
                        a1 = u0 + coarse(kd0, xs + 1, c, ym // 2)[None] + out[c][ym]
                        put_fine(ka1, p, c, ym, a1)
                        d = coarse(kdy, xs + 1, c, ym // 2)[None]
                        put_fine(ky, p, c, ym, y_of(a1, u0, fine(k1, p, c, ym), fine(k2, p, c, ym), d))

            @pl.when(i == 1)
            def _():
                start(xa, (0, 1))

        def part1():
            each(NXC + 2, corrections, 5)
            for side in range(2):
                d0 = ch[ks, side] - ch[kv0, side]
                d2 = ch[ke, side] - ch[kv2, side]
                ch[kdx, side] = 0.375 * d0 + 0.125 * d2
                ch[kdy, side] = 0.125 * (d2 - d0)
            each(NXL + 2, x_plane, 2)
            for side, c, at in halo_blocks():
                d = ch[kdx, side, pl.ds(c * 8, 8), :]
                fh[kx, side, at, :] = x_of(fh[ku0, side, at, :], fh[k1, side, at, :], fh[k2, side, at, :], d)
            each(NXC, first_node)
            pack_fine(ka1)
            start(xa, (2, 3))

        def y_halo_plane(p, xc):
            for c in range(3):
                for ym in range(4):
                    d = coarse(kdy, xc, c, ym // 2)[None]
                    put_fine(ky, p, c, ym, y_of(fine(ka1, p, c, ym), fine(ku0, p, c, ym), fine(k1, p, c, ym), fine(k2, p, c, ym), d))

        def second_node(i):
            xs = edges_first(i)
            planes = []
            for xm in range(2):
                out = rhs(ky, xs, xm)
                p = 2 * xs + xm + 1
                for c in range(3):
                    for ym in range(4):
                        out[c][ym] = fine(ka1, p, c, ym) + out[c][ym]
                        put_fine(ka2, p, c, ym, out[c][ym])
                planes.append(out)
            if mean_of is not None:
                for c in range(3):
                    for ym in range(2):
                        put_coarse(mean_of, xs + 1, c, ym, restricted([q[c] for q in planes], ym) * 0.125)
            if after_edges is not None:
                @pl.when(i == 1)
                def _():
                    after_edges()
            else:
                give(xs).start()

        def part2():
            arrive(xa, (0, 1))
            y_halo_plane(0, 0)
            y_halo_plane(NXL + 1, NXC + 1)
            arrive(xa, (2, 3))
            for side, c, at in halo_blocks():
                d = ch[kdy, side, pl.ds(c * 8, 8), :]
                fh[ky, side, at, :] = y_of(fh[ka1, side, at, :], fh[ku0, side, at, :], fh[k1, side, at, :], fh[k2, side, at, :], d)
            each(NXC, second_node)

        return xa, part1, part2

    arrive(same1)
    xa2 = fine_exchange(A2A, XA2)
    xcv2 = coarse_exchange(CV2, CV2, XCV2)

    def send_edges():
        start(xa2, (0, 1))
        start(xcv2, (0, 1))

    xn = fine_exchange(NEXT, XN)
    xcn = coarse_exchange(CNEXT, CNEXT, XCN)

    def send_next_edges():
        start(xn, (0, 1))
        start(xcn, (0, 1))

    xa1, own1, own2 = sweep(u0_1, v0_1, s_1, CG, CE1, GUESS, GUESS, A1A, A2A, XA1, send_edges, CV2)
    xap, before1, before2 = sweep(START, CSTART, CPS, CSTART, CS1, START, START, A1P, NEXT, XAP, send_next_edges, CNEXT,
                                  WRKP, YBP, CDXP, CDYP, CD0P)
    own1()

    @pl.when(t == 2)
    def _():
        guess_on[2].wait_recv()
        take(raw_rows(2), START, 2, 3)
        pack_fine(START)
        start(xs_)
        means(START, CSTART)
        pack_coarse(CSTART)
        start(xcs)

    own2()
    pack_fine(A2A)
    start(xa2, (2, 3))
    pack_coarse(CV2)
    start(xcv2, (2, 3))

    @pl.when(t == 2)
    def _():
        for copy in before_on:
            copy.wait_recv()
        arrive(xs_)
        arrive(xcs)
        before1()

    whole = pl.ds(FP, NXL * FP)
    bulk = onward(fb.at[A2A, whole], fb.at[NEXT, whole], TU)
    to_z = onward(zout, zin, TZ)
    even = jnp.logical_or(t == 0, t == 2)
    odd = jnp.logical_or(t == 1, t == 3)

    @pl.when(even)
    def _():
        bulk.start()

    restricted_rhs(A1A, 2.0 / 3.0, keep_offset)
    arrive(xa2)
    arrive(xcv2)

    def both(x, c, ym, value):
        at = crow(x, c, ym)
        off[at, :] = off[at, :] + value
        zout[at, :] = value

    restricted_rhs(A2A, 1.0 / 6.0, both)

    def less_end(x):
        out = coarse_rhs(CV2, x)
        for c in range(3):
            for ym in range(2):
                at = crow(x, c, ym)
                zout[at, :] = zout[at, :] - out[c][ym]

    each(NXC, less_end, 4)

    @pl.when(t < 3)
    def _():
        to_z.start()

    @pl.when(t > 0)
    def _():
        to_z.wait_recv()

    def add_previous(x):
        for c in range(3):
            for ym in range(2):
                at = crow(x, c, ym)
                off[at, :] = off[at, :] + zin[at, :]

    each(NXC, add_previous, 4)
    next2, skew2, same2 = chain(CS2, CE2, XS2, XE2, TE2)

    @pl.when(t == 2)
    def _():
        before2()
        pack_fine(NEXT)
        start(xn, (2, 3))
        pack_coarse(CNEXT)
        start(xcn, (2, 3))

    @pl.when(odd)
    def _():
        bulk.wait_recv()
        start(xn, (0, 1))
        pack_fine(NEXT)
        start(xn, (2, 3))
        means(NEXT, CNEXT)
        pack_coarse(CNEXT)
        start(xcn)

    arrive(same2)

    @pl.when(t > 0)
    def _():
        arrive(xn)
        arrive(xcn)

    xb1, own1, own2 = sweep(u0_2, v0_2, s_2, CV2, CE2, A1A, A2A, A1B, WRK, XB1, None, None)
    own1()
    own2()

    for copies in (xv, xg, xcg, same1, xa1, xa2, xcv2, same2, xb1):
        sent(copies)

    @pl.when(even)
    def _():
        sent(xs_)
        sent([bulk])

    @pl.when(t == 1)
    def _():
        sent(guess_on + before_on)

    @pl.when(t == 2)
    def _():
        sent(xcs)
        sent(xap)

    @pl.when(t > 0)
    def _():
        sent(xn)
        sent(xcn)

    @pl.when(t < 3)
    def _():
        for copies in (skew1, skew2, [next1, next2, to_z]):
            sent(copies)

    for xs in range(NXC):
        give(xs).wait()


def reorder(rows_hbm, out_hbm, rows, halves, insem, outsem):
    chunks = NXL // PLANES
    size = PLANES * FP

    def get(i):
        at = pl.ds(i * size, size)
        return pltpu.make_async_copy(rows_hbm.at[at], rows.at[at], insem.at[i])

    def put(i, h):
        return pltpu.make_async_copy(
            halves.at[h, :, pl.ds(i * PLANES, PLANES)],
            out_hbm.at[0, :, pl.ds(i * PLANES, PLANES), :, pl.ds(h * 128, 128)], outsem.at[i, h])

    for i in range(chunks):
        get(i).start()
    row_i = lax.broadcasted_iota(jnp.int32, (256, 256), 0)
    col_i = lax.broadcasted_iota(jnp.int32, (256, 256), 1)
    back = (col_i == 2 * lax.rem(row_i, 128) + row_i // 128).astype(jnp.bfloat16)
    for i in range(chunks):
        get(i).wait()
        for c in range(3):
            blocks = []
            for xx in range(PLANES):
                for ym in range(4):
                    at = i * size + xx * FP + (c * 4 + ym) * 16
                    blocks.append(jnp.concatenate([rows[pl.ds(at + 8 * zm, 8), :] for zm in range(2)], axis=1))
            got = permute(jnp.concatenate(blocks, axis=0), back)
            for xx in range(PLANES):
                for ym in range(4):
                    row = (xx * 4 + ym) * 8
                    for h in range(2):
                        halves[h, c, i * PLANES + xx, pl.ds(ym, 8, stride=4), :] = got[row : row + 8, h * 128 : (h + 1) * 128]
        for h in range(2):
            put(i, h).start()
    for i in range(chunks):
        for h in range(2):
            put(i, h).wait()


def shards(velocity, start_field, guess):
    anywhere = pl.BlockSpec(memory_space=pl.ANY)
    rows = pl.pallas_call(
        kernel,
        out_shape=jax.ShapeDtypeStruct((NXL * FP, 128), F32),
        in_specs=[anywhere] * 3,
        out_specs=anywhere,
        scratch_shapes=[
            pltpu.VMEM((3, 3, 2, NXL, NYL, 128), F32),
            pltpu.VMEM((NF, (NXL + 2) * FP, 128), F32),
            pltpu.VMEM((NXL * 9 * 64, 128), F32),
            pltpu.VMEM((NF, 2, 96, 128), F32),
            pltpu.VMEM((NF, 2, 96, 128), F32),
            pltpu.VMEM((NC, (NXC + 2) * CP, 128), F32),
            pltpu.VMEM((NXC * CP, 128), F32),
            pltpu.VMEM((NXC * 144, 128), F32),
            pltpu.VMEM((NC, 2, 24, 128), F32),
            pltpu.VMEM((NC, 2, 24, 128), F32),
            pltpu.VMEM((NXC * CP, 128), F32),
            pltpu.VMEM((NXC * CP, 128), F32),
            pltpu.VMEM((NXC * CP, 128), F32),
            pltpu.SemaphoreType.DMA((3, 2)),
            pltpu.SemaphoreType.DMA((NXC,)),
            pltpu.SemaphoreType.DMA((NX_, 4)),
            pltpu.SemaphoreType.DMA((NX_, 4)),
            pltpu.SemaphoreType.DMA((NT,)),
            pltpu.SemaphoreType.DMA((NT,)),
        ],
        compiler_params=pltpu.CompilerParams(
            collective_id=0, has_side_effects=True, vmem_limit_bytes=60 * 1024 * 1024
        ),
        name="pfasst",
    )(velocity, start_field, guess)
    chunks = NXL // PLANES
    return pl.pallas_call(
        reorder,
        out_shape=jax.ShapeDtypeStruct((1, 3, NXL, NYL, NZL), F32),
        in_specs=[anywhere],
        out_specs=anywhere,
        scratch_shapes=[
            pltpu.VMEM((NXL * FP, 128), F32),
            pltpu.VMEM((2, 3, NXL, NYL, 128), F32),
            pltpu.SemaphoreType.DMA((chunks,)),
            pltpu.SemaphoreType.DMA((chunks, 2)),
        ],
        name="reorder",
    )(rows)


def solution(mesh):
    in_specs = (
        P(None, "gx", "gy", None),
        P(None, "gx", "gy", None),
        P("tm", None, "gx", "gy", None),
    )
    out_specs = P("tm", None, "gx", "gy", None)
    return jax.shard_map(shards, mesh=mesh, in_specs=in_specs, out_specs=out_specs, check_vma=False)
```

```python
import jax
import jax.numpy as jnp
from jax import lax
from jax.experimental import pallas as pl
from jax.experimental.pallas import tpu as pltpu
from jax.sharding import PartitionSpec as P


MESH = pl.DeviceIdType.MESH
F32 = jnp.float32
NU = 0.125
NUC = 0.03125
FP, CP = 192, 48
NXL, NYL, NZL = 16, 32, 256
NXC = NXL // 2
GUESS, START, NEXT, A1A, A2A, A1B, WRK, YB, VEL, A1P, WRKP, YBP, SUM = range(13)
NF = 13
CG, CSTART, CNEXT, CV2, CS1, CS2, CE1, CE2, CPS, CDX, CDY, CD0, CDXP, CDYP, CD0P = range(15)
NC = 15
XV, XG, XS, XCG, XCS, XS1, XE1, XA1, XA2, XCV2, XN, XCN, XS2, XE2, XB1, XW, XAP = range(17)
NX_ = 17
TE1, TE2, TZ, TU, TP, TPH, TG = range(7)
NT = TG + 4
PLANES = 4


def split3(v):
    hi = v.astype(jnp.bfloat16)
    rest = v - hi.astype(F32)
    mid = rest.astype(jnp.bfloat16)
    low = (rest - mid.astype(F32)).astype(jnp.bfloat16)
    return hi, mid, low


def permute(v, table):
    parts = [jnp.dot(p, table, preferred_element_type=F32) for p in split3(v)]
    return parts[0] + parts[1] + parts[2]


def kernel(vel_hbm, start_hbm, guess_hbm, out_hbm, raw, fb, gd, fh, fpk, cb, hvc, gc, ch, cpk, off, zin, zout,
           insem, outsem, xss, xrs, tss, trs):
    t, gx, gy = lax.axis_index("tm"), lax.axis_index("gx"), lax.axis_index("gy")
    first = t == 0
    gxm, gxp = lax.rem(gx + 7, 8), lax.rem(gx + 1, 8)
    gym, gyp = lax.rem(gy + 3, 4), lax.rem(gy + 1, 4)
    around = ((gxm, gy), (gxp, gy), (gx, gym), (gx, gyp))
    sub = lax.broadcasted_iota(jnp.int32, (2, 8, 128), 1)
    subc = lax.broadcasted_iota(jnp.int32, (8, 128), 0)
    row_i = lax.broadcasted_iota(jnp.int32, (256, 256), 0)
    col_i = lax.broadcasted_iota(jnp.int32, (256, 256), 1)

    def load(hbm, which):
        return [
            pltpu.make_async_copy(hbm.at[:, :, :, pl.ds(h * 128, 128)], raw.at[which, :, h], insem.at[which, h])
            for h in range(2)
        ]

    ins = [load(vel_hbm, 0), load(guess_hbm.at[0], 1), load(start_hbm, 2)]
    for copy in ins[0] + ins[1]:
        copy.start()

    @pl.when(first)
    def _():
        for copy in ins[2]:
            copy.start()

    bar = pltpu.get_barrier_semaphore()
    for ox, oy in around:
        pl.semaphore_signal(bar, inc=1, device_id=(t, ox, oy), device_id_type=MESH)

    @pl.when(t > 0)
    def _():
        pl.semaphore_signal(bar, inc=1, device_id=(t - 1, gx, gy), device_id_type=MESH)

    def exchange(src, dst, pack, halo, which, planes, size, dt=0):
        far = planes * size
        parts = (
            (src.at[pl.ds(size, size)], dst.at[pl.ds(far + size, size)]),
            (src.at[pl.ds(far, size)], dst.at[pl.ds(0, size)]),
            (pack.at[0], halo.at[1]),
            (pack.at[1], halo.at[0]),
        )
        return [
            pltpu.make_async_remote_copy(
                src_ref=s, dst_ref=d, send_sem=xss.at[which, i], recv_sem=xrs.at[which, i],
                device_id=(t + dt, around[i][0], around[i][1]), device_id_type=MESH)
            for i, (s, d) in enumerate(parts)
        ]

    def fine_exchange(k, which):
        return exchange(fb.at[k], fb.at[k], fpk.at[k], fh.at[k], which, NXL, FP)

    def coarse_exchange(k, dst, which, dt=0):
        return exchange(cb.at[k], cb.at[dst], cpk.at[k], ch.at[dst], which, NXC, CP, dt)

    def onward(src, dst, which):
        return pltpu.make_async_remote_copy(
            src_ref=src, dst_ref=dst, send_sem=tss.at[which], recv_sem=trs.at[which],
            device_id=(t + 1, gx, gy), device_id_type=MESH)

    def start(copies, which=(0, 1, 2, 3)):
        for i in which:
            copies[i].start()

    def arrive(copies, which=(0, 1, 2, 3)):
        for i in which:
            copies[i].wait_recv()

    def sent(copies):
        for copy in copies:
            copy.wait_send()

    def fine(k, plane, c, ym):
        return fb[k, pl.ds(pl.multiple_of(plane * FP + (c * 4 + ym) * 16, 16), 16), :].reshape(2, 8, 128)

    def put_fine(k, plane, c, ym, value):
        fb[k, pl.ds(pl.multiple_of(plane * FP + (c * 4 + ym) * 16, 16), 16), :] = value.reshape(16, 128)

    def coarse(k, plane, c, ym):
        return cb[k, pl.ds(pl.multiple_of(plane * CP + (c * 2 + ym) * 8, 8), 8), :]

    def put_coarse(k, plane, c, ym, value):
        cb[k, pl.ds(pl.multiple_of(plane * CP + (c * 2 + ym) * 8, 8), 8), :] = value

    def pack_fine(k):
        for c in range(3):
            for zm in range(2):
                for xm in range(2):
                    at = FP * (1 + xm) + c * 64 + zm * 8
                    to = ((c * 2 + zm) * 2 + xm) * 8
                    fpk[k, 0, pl.ds(to, 8), :] = fb[k, pl.ds(at, 8, stride=2 * FP), :]
                    fpk[k, 1, pl.ds(to, 8), :] = fb[k, pl.ds(at + 48 + 7, 8, stride=2 * FP), :]

    def pack_coarse(k):
        for c in range(3):
            at = CP + c * 16
            cpk[k, 0, pl.ds(c * 8, 8), :] = cb[k, pl.ds(at, 8, stride=CP), :]
            cpk[k, 1, pl.ds(c * 8, 8), :] = cb[k, pl.ds(at + 8 + 7, 8, stride=CP), :]

    def halo_rows(k, side, c, xs, xm):
        rows = [
            jnp.broadcast_to(fh[k, side, pl.ds(((c * 2 + zm) * 2 + xm) * 8 + xs, 1), :], (8, 128)) for zm in range(2)
        ]
        return jnp.stack(rows)

    def halo_row(k, side, c, x):
        return jnp.broadcast_to(ch[k, side, pl.ds(c * 8 + x, 1), :], (8, 128))

    def y_ahead(w, k, c, ym, xs, xm):
        if ym < 3:
            return w[ym + 1]
        if xm is None:
            return jnp.where(sub == 7, 0.0, pltpu.roll(w[0], 7, axis=1))
        return jnp.where(sub == 7, halo_rows(k, 1, c, xs, xm), pltpu.roll(w[0], 7, axis=1))

    def y_behind(w, k, c, ym, xs, xm):
        if ym > 0:
            return w[ym - 1]
        if xm is None:
            return jnp.where(sub == 0, 0.0, pltpu.roll(w[3], 1, axis=1))
        return jnp.where(sub == 0, halo_rows(k, 0, c, xs, xm), pltpu.roll(w[3], 1, axis=1))

    def z_ahead(v):
        return jnp.concatenate([v[1:2], pltpu.roll(v[0:1], 127, axis=2)], axis=0)

    def z_behind(v):
        return jnp.concatenate([pltpu.roll(v[1:2], 1, axis=2), v[0:1]], axis=0)

    def restricted(planes, ym):
        total = planes[0][2 * ym] + planes[0][2 * ym + 1] + planes[1][2 * ym] + planes[1][2 * ym + 1]
        return total[0] + total[1]

    def rhs(k, xs, xm, halo=True):
        x = 2 * xs + xm
        if not halo:
            xm = None
        w = [[fine(k, x + 1, c, ym) for ym in range(4)] for c in range(3)]
        out = [[None] * 4 for _ in range(3)]
        for ym in range(4):
            v = [fine(VEL, x + 1, b, ym) for b in range(3)]
            ahead = [NU - q for q in v]
            behind = [NU + q for q in v]
            for c in range(3):
                total = ahead[0] * fine(k, x + 2, c, ym) + behind[0] * fine(k, x, c, ym)
                total += ahead[1] * y_ahead(w[c], k, c, ym, xs, xm)
                total += behind[1] * y_behind(w[c], k, c, ym, xs, xm)
                total += ahead[2] * z_ahead(w[c][ym])
                total += behind[2] * z_behind(w[c][ym])
                for b in range(3):
                    at = x * (9 * 64) + ((3 * c + b) * 4 + ym) * 16
                    total += w[b][ym] * gd[pl.ds(pl.multiple_of(at, 16), 16), :].reshape(2, 8, 128)
                out[c][ym] = total
        return out

    def coarse_rhs(k, x):
        w = [[coarse(k, x + 1, c, ym) for ym in range(2)] for c in range(3)]
        out = [[None] * 2 for _ in range(3)]
        for ym in range(2):
            v = [hvc[pl.ds(pl.multiple_of(x * CP + (b * 2 + ym) * 8, 8), 8), :] for b in range(3)]
            ahead = [NUC - q for q in v]
            behind = [NUC + q for q in v]
            for c in range(3):
                if ym == 0:
                    ya = w[c][1]
                    yb = jnp.where(subc == 0, halo_row(k, 0, c, x), pltpu.roll(w[c][1], 1, axis=0))
                else:
                    ya = jnp.where(subc == 7, halo_row(k, 1, c, x), pltpu.roll(w[c][0], 7, axis=0))
                    yb = w[c][0]
                total = ahead[0] * coarse(k, x + 2, c, ym) + behind[0] * coarse(k, x, c, ym)
                total += ahead[1] * ya + behind[1] * yb
                total += ahead[2] * pltpu.roll(w[c][ym], 127, axis=1) + behind[2] * pltpu.roll(w[c][ym], 1, axis=1)
                for b in range(3):
                    at = x * 144 + ((3 * c + b) * 2 + ym) * 8
                    total += w[b][ym] * gc[pl.ds(pl.multiple_of(at, 8), 8), :]
                out[c][ym] = total
        return out

    def each(count, body, unroll=1):
        lax.fori_loop(0, count, lambda i, carry: (body(i), carry)[1], 0, unroll=unroll)

    def crow(x, c, ym):
        return pl.ds(pl.multiple_of(x * CP + (c * 2 + ym) * 8, 8), 8)

    def edges_first(i):
        return jnp.where(i == 0, 0, jnp.where(i == 1, NXC - 1, i - 1))

    def restricted_rhs(k, scale, use):
        def body(xs):
            planes = [rhs(k, xs, xm) for xm in range(2)]
            for c in range(3):
                for ym in range(2):
                    use(xs, c, ym, restricted([p[c] for p in planes], ym) * (scale / 8.0))

        each(NXC, body)

    table = (row_i == 2 * lax.rem(col_i, 128) + col_i // 128).astype(jnp.bfloat16)

    def take(read, k, c_from=0, c_to=3):
        def body(i):
            c, xq = i // 4, lax.rem(i, 4)
            got = permute(read(c, xq), table)
            for xx in range(4):
                for ym in range(4):
                    for zm in range(2):
                        at = (xq * 4 + xx + 1) * FP + c * 64 + (ym * 2 + zm) * 8
                        row = (xx * 4 + ym) * 8
                        fb[k, pl.ds(pl.multiple_of(at, 8), 8), :] = got[row : row + 8, zm * 128 : (zm + 1) * 128]

        lax.fori_loop(4 * c_from, 4 * c_to, lambda i, carry: (body(i), carry)[1], 0, unroll=2)

    def raw_rows(which):
        def read(c, xq):
            blocks = []
            for xx in range(4):
                for ym in range(4):
                    rows = [raw[which, c, h, xq * 4 + xx, pl.ds(ym, 8, stride=4), :] for h in range(2)]
                    blocks.append(jnp.concatenate(rows, axis=1))
            return jnp.concatenate(blocks, axis=0)

        return read

    def means(k, ck):
        def body(xs):
            for c in range(3):
                planes = [[fine(k, 2 * xs + xm + 1, c, ym) for ym in range(4)] for xm in range(2)]
                for ym in range(2):
                    put_coarse(ck, xs + 1, c, ym, restricted(planes, ym) * 0.125)

        each(NXC, body, 2)

    xv = fine_exchange(VEL, XV)
    xw = fine_exchange(SUM, XW)
    xg = fine_exchange(GUESS, XG)
    xs_ = fine_exchange(START, XS)
    xcg = coarse_exchange(CG, CG, XCG)

    guess_on = [
        onward(guess_hbm.at[0, 0, :, :, pl.ds(h * 128, 128)], raw.at[2, 0, h], TG + h) for h in range(2)
    ] + [onward(raw.at[1, c], raw.at[2, c], TG + 1 + c) for c in (1, 2)]

    @pl.when(t == 1)
    def _():
        pl.semaphore_wait(bar, 5)
        guess_on[0].start()
        guess_on[1].start()

    for k in (WRK, YB, WRKP, YBP):
        for plane in (0, NXL + 1):
            fb[k, pl.ds(plane * FP, FP), :] = jnp.zeros((FP, 128), F32)
    for copy in ins[0]:
        copy.wait()
    take(lambda c, xq: raw_rows(0)(c, xq) * 0.25, VEL)
    pack_fine(VEL)

    @pl.when(jnp.logical_or(t == 0, t == 2))
    def _():
        pl.semaphore_wait(bar, 5)

    @pl.when(t == 3)
    def _():
        pl.semaphore_wait(bar, 4)

    start(xv)
    for copy in ins[1]:
        copy.wait()
    @pl.when(first)
    def _():
        for copy in ins[2]:
            copy.wait()
        take(lambda c, xq: raw_rows(2)(c, xq) * (1.0 / 6.0) + raw_rows(1)(c, xq) * (5.0 / 6.0), SUM)
        pack_fine(SUM)
        start(xw)

    take(raw_rows(1), GUESS)
    pack_fine(GUESS)
    start(xg)
    means(GUESS, CG)
    pack_coarse(CG)
    start(xcg)

    @pl.when(t == 1)
    def _():
        guess_on[2].start()

    @pl.when(first)
    def _():
        take(raw_rows(2), START)
        pack_fine(START)
        start(xs_)
        means(START, CSTART)
        for side in range(2):
            ch[CSTART, side] = jnp.zeros((24, 128), F32)
            cb[CSTART, pl.ds(side * (NXC + 1) * CP, CP), :] = jnp.zeros((CP, 128), F32)

    arrive(xv)

    def gradients(xs):
        for a in range(3):
            kept = [[None, None] for _ in range(3)]
            vel = [None, None]
            for xm in range(2):
                x = 2 * xs + xm
                w = [fine(VEL, x + 1, a, ym) for ym in range(4)]
                vel[xm] = w
                diffs = [[None] * 4 for _ in range(3)]
                for ym in range(4):
                    diffs[0][ym] = fine(VEL, x + 2, a, ym) - fine(VEL, x, a, ym)
                    diffs[1][ym] = y_ahead(w, VEL, a, ym, xs, xm) - y_behind(w, VEL, a, ym, xs, xm)
                    diffs[2][ym] = z_ahead(w[ym]) - z_behind(w[ym])
                for b in range(3):
                    for ym in range(4):
                        if a == b:
                            diffs[b][ym] = diffs[b][ym] - 6.0 * NU
                        at = x * (9 * 64) + ((3 * a + b) * 4 + ym) * 16
                        gd[pl.ds(pl.multiple_of(at, 16), 16), :] = diffs[b][ym].reshape(16, 128)
                    kept[b][xm] = diffs[b]
            for ym in range(2):
                hvc[crow(xs, a, ym), :] = restricted(vel, ym) * 0.0625
                for b in range(3):
                    at = xs * 144 + ((3 * a + b) * 2 + ym) * 8
                    mean = restricted(kept[b], ym) * 0.125
                    if a == b:
                        mean = mean + 6.0 * (NU - NUC)
                    gc[pl.ds(pl.multiple_of(at, 8), 8), :] = mean

    each(NXC, gradients)

    @pl.when(first)
    def _():
        arrive(xw)

    @pl.when(t > 0)
    def _():
        arrive(xg)
        arrive(xcg)

    def keep_offset(x, c, ym, value):
        off[crow(x, c, ym), :] = value

    restricted_rhs(jnp.where(first, SUM, GUESS), 1.0, keep_offset)

    u0_1 = jnp.where(first, START, GUESS)
    u0_2 = jnp.where(first, START, NEXT)
    v0_1 = jnp.where(first, CSTART, CG)
    v0_2 = jnp.where(first, CSTART, CNEXT)
    s_1 = jnp.where(first, CSTART, CS1)
    s_2 = jnp.where(first, CSTART, CS2)

    @pl.when(t > 0)
    def _():
        def less_start(x):
            out = coarse_rhs(CG, x)
            for c in range(3):
                for ym in range(2):
                    at = crow(x, c, ym)
                    off[at, :] = off[at, :] - out[c][ym]

        each(NXC, less_start, 4)

    inner = pl.ds(CP, NXC * CP)

    def chain(ks, ke, xs_id, xe_id, te):
        to_next = onward(cb.at[ke, inner], cb.at[{CE1: CS1, CE2: CS2}[ke], inner], te)
        skew = coarse_exchange(ke, {CE1: CS1, CE2: CS2}[ke], xs_id, 1)
        same = coarse_exchange(ke, ke, xe_id)

        @pl.when(t > 0)
        def _():
            arrive(skew)
            to_next.wait_recv()

            def body(x):
                out = coarse_rhs(ks, x)
                for c in range(3):
                    for ym in range(2):
                        put_coarse(ke, x + 1, c, ym, coarse(ks, x + 1, c, ym) + out[c][ym] + off[crow(x, c, ym), :])

            each(NXC, body, 4)

        @pl.when(first)
        def _():
            def body(x):
                for c in range(3):
                    for ym in range(2):
                        put_coarse(ke, x + 1, c, ym, coarse(CSTART, x + 1, c, ym) + off[crow(x, c, ym), :])

            each(NXC, body, 4)

        pack_coarse(ke)

        @pl.when(t < 3)
        def _():
            start(skew)
            to_next.start()

        start(same)
        return to_next, skew, same

    xcs = coarse_exchange(CSTART, CSTART, XCS)

    @pl.when(t == 2)
    def _():
        for copy in guess_on[:3]:
            copy.wait_recv()
        take(raw_rows(2), START, 0, 2)

    next1, skew1, same1 = chain(CS1, CE1, XS1, XE1, TE1)

    before_on = [onward(cb.at[CS1], cb.at[CPS], TP), onward(ch.at[CS1], ch.at[CPS], TPH)]

    @pl.when(t == 1)
    def _():
        for copy in before_on + [guess_on[3]]:
            copy.start()

    @pl.when(first)
    def _():
        arrive(xs_)
        arrive(xg)
        arrive(xcg)

        def keep(x, c, ym, value):
            zin[crow(x, c, ym), :] = value

        restricted_rhs(START, 1.0 / 6.0, keep)

    def give(xs):
        at = pl.ds(pl.multiple_of(xs * 2 * FP, 2 * FP), 2 * FP)
        return pltpu.make_async_copy(fb.at[WRK, pl.ds(pl.multiple_of(xs * 2 * FP + FP, FP), 2 * FP)], out_hbm.at[at], outsem.at[xs])

    def sweep(ku0, kv0, ks, kv2, ke, k1, k2, ka1, ka2, xa_id, halos_in, mean_of, kx=WRK, ky=YB, kdx=CDX, kdy=CDY, kd0=CD0):
        def corrections(x):
            for c in range(3):
                for ym in range(2):
                    d0 = coarse(ks, x, c, ym) - coarse(kv0, x, c, ym)
                    d2 = coarse(ke, x, c, ym) - coarse(kv2, x, c, ym)
                    put_coarse(kd0, x, c, ym, d0)
                    put_coarse(kdx, x, c, ym, 0.375 * d0 + 0.125 * d2)
                    put_coarse(kdy, x, c, ym, 0.125 * (d2 - d0))

        def x_of(u0, u1, u2, d):
            if k1 == k2:
                return (5.0 / 24.0) * u0 + (7.0 / 24.0) * u1 + d
            return (5.0 / 24.0) * u0 + (1.0 / 3.0) * u1 - (1.0 / 24.0) * u2 + d

        def y_of(a1, u0, u1, u2, d):
            if k1 == k2:
                return 0.5 * a1 - (1.0 / 24.0) * u0 + (1.0 / 24.0) * u1 + d
            return 0.5 * a1 - (1.0 / 24.0) * u0 - (1.0 / 6.0) * u1 + (5.0 / 24.0) * u2 + d

        def x_plane(i):
            p = i + 1
            xc = (p + 1) // 2
            for c in range(3):
                for ym in range(4):
                    d = coarse(kdx, xc, c, ym // 2)[None]
                    put_fine(kx, p, c, ym, x_of(fine(ku0, p, c, ym), fine(k1, p, c, ym), fine(k2, p, c, ym), d))

        xa = fine_exchange(ka1, xa_id)

        def first_node(xs):
            for xm in range(2):
                out = rhs(kx, xs, xm, False)
                p = 2 * xs + xm + 1
                for c in range(3):
                    for ym in range(4):
                        u0 = fine(ku0, p, c, ym)
                        a1 = u0 + coarse(kd0, xs + 1, c, ym // 2)[None] + out[c][ym]
                        put_fine(ka1, p, c, ym, a1)
                        d = coarse(kdy, xs + 1, c, ym // 2)[None]
                        put_fine(ky, p, c, ym, y_of(a1, u0, fine(k1, p, c, ym), fine(k2, p, c, ym), d))

        def second_node(xs):
            planes = []
            for xm in range(2):
                out = rhs(ky, xs, xm, False)
                p = 2 * xs + xm + 1
                for c in range(3):
                    for ym in range(4):
                        out[c][ym] = fine(ka1, p, c, ym) + out[c][ym]
                        put_fine(ka2, p, c, ym, out[c][ym])
                planes.append(out)
            if mean_of is not None:
                for c in range(3):
                    for ym in range(2):
                        put_coarse(mean_of, xs + 1, c, ym, restricted([q[c] for q in planes], ym) * 0.125)

        x_sides = ((0, 1, 0, 1), (NXL + 1, NXL, NXC + 1, NXC))

        def coefficient(side, v):
            return NU + v if side == 0 else NU - v

        def blocks(side):
            for c in range(3):
                for zm in range(2):
                    for xm in range(2):
                        at = FP * (1 + xm) + c * 64 + zm * 8 + side * 55
                        yield c, pl.ds(at, 8, stride=2 * FP), pl.ds(((c * 2 + zm) * 2 + xm) * 8, 8), pl.ds(((2 + zm) * 2 + xm) * 8, 8)

        def part1():
            each(NXC, lambda x: corrections(x + 1), 4)
            each(NXL, x_plane, 2)
            each(NXC, first_node)
            halos_in()
            for side, (far, edge, cfar, _) in enumerate(x_sides):
                corrections(cfar)
                for ym in range(4):
                    v = coefficient(side, fine(VEL, edge, 0, ym))
                    for c in range(3):
                        d = coarse(kdx, cfar, c, ym // 2)[None]
                        add = v * x_of(fine(ku0, far, c, ym), fine(k1, far, c, ym), fine(k2, far, c, ym), d)
                        put_fine(ka1, edge, c, ym, fine(ka1, edge, c, ym) + add)
                        put_fine(ky, edge, c, ym, fine(ky, edge, c, ym) + 0.5 * add)
            for side in range(2):
                d0 = ch[ks, side] - ch[kv0, side]
                d2 = ch[ke, side] - ch[kv2, side]
                ch[kdx, side] = 0.375 * d0 + 0.125 * d2
                ch[kdy, side] = 0.125 * (d2 - d0)
                for c, rows, at, vat in blocks(side):
                    d = ch[kdx, side, pl.ds(c * 8, 8), :]
                    far = x_of(fh[ku0, side, at, :], fh[k1, side, at, :], fh[k2, side, at, :], d)
                    add = coefficient(side, fpk[VEL, side, vat, :]) * far
                    value = fb[ka1, rows, :] + add
                    fb[ka1, rows, :] = value
                    fpk[ka1, side, at, :] = value
                    fb[ky, rows, :] = fb[ky, rows, :] + 0.5 * add
            start(xa)

        def part2():
            each(NXC, second_node)
            arrive(xa)
            for side, (far, edge, cfar, cedge) in enumerate(x_sides):
                adds = [[None] * 4 for _ in range(3)]
                for ym in range(4):
                    v = coefficient(side, fine(VEL, edge, 0, ym))
                    for c in range(3):
                        d = coarse(kdy, cfar, c, ym // 2)[None]
                        adds[c][ym] = v * y_of(fine(ka1, far, c, ym), fine(ku0, far, c, ym), fine(k1, far, c, ym), fine(k2, far, c, ym), d)
                        put_fine(ka2, edge, c, ym, fine(ka2, edge, c, ym) + adds[c][ym])
                if mean_of is not None:
                    for c in range(3):
                        for ym in range(2):
                            both = adds[c][2 * ym] + adds[c][2 * ym + 1]
                            put_coarse(mean_of, cedge, c, ym, coarse(mean_of, cedge, c, ym) + (both[0] + both[1]) * 0.125)
            for side in range(2):
                means_add = [None] * 3
                for c, rows, at, vat in blocks(side):
                    d = ch[kdy, side, pl.ds(c * 8, 8), :]
                    far = y_of(fh[ka1, side, at, :], fh[ku0, side, at, :], fh[k1, side, at, :], fh[k2, side, at, :], d)
                    add = coefficient(side, fpk[VEL, side, vat, :]) * far
                    value = fb[ka2, rows, :] + add
                    fb[ka2, rows, :] = value
                    fpk[ka2, side, at, :] = value
                    means_add[c] = add if means_add[c] is None else means_add[c] + add
                if mean_of is not None:
                    for c in range(3):
                        rows = pl.ds(CP + c * 16 + side * 15, 8, stride=CP)
                        value = cb[mean_of, rows, :] + means_add[c] * 0.125
                        cb[mean_of, rows, :] = value
                        cpk[mean_of, side, pl.ds(c * 8, 8), :] = value

        return xa, part1, part2

    xa2 = fine_exchange(A2A, XA2)
    xcv2 = coarse_exchange(CV2, CV2, XCV2)
    xn = fine_exchange(NEXT, XN)
    xcn = coarse_exchange(CNEXT, CNEXT, XCN)

    def before_in():
        arrive(xs_)
        arrive(xcs)

    xa1, own1, own2 = sweep(u0_1, v0_1, s_1, CG, CE1, GUESS, GUESS, A1A, A2A, XA1, lambda: arrive(same1), CV2)
    xap, before1, before2 = sweep(START, CSTART, CPS, CSTART, CS1, START, START, A1P, NEXT, XAP, before_in, CNEXT,
                                  WRKP, YBP, CDXP, CDYP, CD0P)
    own1()

    @pl.when(t == 2)
    def _():
        guess_on[3].wait_recv()
        take(raw_rows(2), START, 2, 3)
        pack_fine(START)
        start(xs_)
        means(START, CSTART)
        pack_coarse(CSTART)
        start(xcs)

    own2()
    start(xa2)
    start(xcv2)

    @pl.when(t == 2)
    def _():
        for copy in before_on:
            copy.wait_recv()
        before1()

    whole = pl.ds(FP, NXL * FP)
    bulk = onward(fb.at[A2A, whole], fb.at[NEXT, whole], TU)
    to_z = onward(zout, zin, TZ)
    even = jnp.logical_or(t == 0, t == 2)
    odd = jnp.logical_or(t == 1, t == 3)

    @pl.when(even)
    def _():
        bulk.start()

    restricted_rhs(A1A, 2.0 / 3.0, keep_offset)
    arrive(xa2)
    arrive(xcv2)

    def both(x, c, ym, value):
        at = crow(x, c, ym)
        off[at, :] = off[at, :] + value
        zout[at, :] = value

    restricted_rhs(A2A, 1.0 / 6.0, both)

    def less_end(x):
        out = coarse_rhs(CV2, x)
        for c in range(3):
            for ym in range(2):
                at = crow(x, c, ym)
                zout[at, :] = zout[at, :] - out[c][ym]

    each(NXC, less_end, 4)

    @pl.when(t < 3)
    def _():
        to_z.start()

    @pl.when(t > 0)
    def _():
        to_z.wait_recv()

    def add_previous(x):
        for c in range(3):
            for ym in range(2):
                at = crow(x, c, ym)
                off[at, :] = off[at, :] + zin[at, :]

    each(NXC, add_previous, 4)
    next2, skew2, same2 = chain(CS2, CE2, XS2, XE2, TE2)

    @pl.when(t == 2)
    def _():
        before2()
        start(xn)
        start(xcn)

    @pl.when(odd)
    def _():
        bulk.wait_recv()
        start(xn, (0, 1))
        pack_fine(NEXT)
        start(xn, (2, 3))
        means(NEXT, CNEXT)
        pack_coarse(CNEXT)
        start(xcn)

    def second_in():
        arrive(same2)

        @pl.when(t > 0)
        def _():
            arrive(xn)
            arrive(xcn)

    xb1, own1, own2 = sweep(u0_2, v0_2, s_2, CV2, CE2, A1A, A2A, A1B, WRK, XB1, second_in, None)
    own1()
    own2()
    for xs in range(NXC):
        give(xs).start()

    for copies in (xv, xg, xcg, same1, xa1, xa2, xcv2, same2, xb1):
        sent(copies)

    @pl.when(first)
    def _():
        sent(xw)

    @pl.when(even)
    def _():
        sent(xs_)
        sent([bulk])

    @pl.when(t == 1)
    def _():
        sent(guess_on + before_on)

    @pl.when(t == 2)
    def _():
        sent(xcs)
        sent(xap)

    @pl.when(t > 0)
    def _():
        sent(xn)
        sent(xcn)

    @pl.when(t < 3)
    def _():
        for copies in (skew1, skew2, [next1, next2, to_z]):
            sent(copies)

    for xs in range(NXC):
        give(xs).wait()


def reorder(rows_hbm, out_hbm, rows, halves, insem, outsem):
    chunks = NXL // PLANES
    size = PLANES * FP

    def get(i):
        at = pl.ds(i * size, size)
        return pltpu.make_async_copy(rows_hbm.at[at], rows.at[at], insem.at[i])

    def put(i, h):
        return pltpu.make_async_copy(
            halves.at[h, :, pl.ds(i * PLANES, PLANES)],
            out_hbm.at[0, :, pl.ds(i * PLANES, PLANES), :, pl.ds(h * 128, 128)], outsem.at[i, h])

    for i in range(chunks):
        get(i).start()
    row_i = lax.broadcasted_iota(jnp.int32, (256, 256), 0)
    col_i = lax.broadcasted_iota(jnp.int32, (256, 256), 1)
    back = (col_i == 2 * lax.rem(row_i, 128) + row_i // 128).astype(jnp.bfloat16)
    for i in range(chunks):
        get(i).wait()
        for c in range(3):
            blocks = []
            for xx in range(PLANES):
                for ym in range(4):
                    at = i * size + xx * FP + (c * 4 + ym) * 16
                    blocks.append(jnp.concatenate([rows[pl.ds(at + 8 * zm, 8), :] for zm in range(2)], axis=1))
            got = permute(jnp.concatenate(blocks, axis=0), back)
            for xx in range(PLANES):
                for ym in range(4):
                    row = (xx * 4 + ym) * 8
                    for h in range(2):
                        halves[h, c, i * PLANES + xx, pl.ds(ym, 8, stride=4), :] = got[row : row + 8, h * 128 : (h + 1) * 128]
        for h in range(2):
            put(i, h).start()
    for i in range(chunks):
        for h in range(2):
            put(i, h).wait()


def shards(velocity, start_field, guess):
    anywhere = pl.BlockSpec(memory_space=pl.ANY)
    rows = pl.pallas_call(
        kernel,
        out_shape=jax.ShapeDtypeStruct((NXL * FP, 128), F32),
        in_specs=[anywhere] * 3,
        out_specs=anywhere,
        scratch_shapes=[
            pltpu.VMEM((3, 3, 2, NXL, NYL, 128), F32),
            pltpu.VMEM((NF, (NXL + 2) * FP, 128), F32),
            pltpu.VMEM((NXL * 9 * 64, 128), F32),
            pltpu.VMEM((NF, 2, 96, 128), F32),
            pltpu.VMEM((NF, 2, 96, 128), F32),
            pltpu.VMEM((NC, (NXC + 2) * CP, 128), F32),
            pltpu.VMEM((NXC * CP, 128), F32),
            pltpu.VMEM((NXC * 144, 128), F32),
            pltpu.VMEM((NC, 2, 24, 128), F32),
            pltpu.VMEM((NC, 2, 24, 128), F32),
            pltpu.VMEM((NXC * CP, 128), F32),
            pltpu.VMEM((NXC * CP, 128), F32),
            pltpu.VMEM((NXC * CP, 128), F32),
            pltpu.SemaphoreType.DMA((3, 2)),
            pltpu.SemaphoreType.DMA((NXC,)),
            pltpu.SemaphoreType.DMA((NX_, 4)),
            pltpu.SemaphoreType.DMA((NX_, 4)),
            pltpu.SemaphoreType.DMA((NT,)),
            pltpu.SemaphoreType.DMA((NT,)),
        ],
        compiler_params=pltpu.CompilerParams(
            collective_id=0, has_side_effects=True, vmem_limit_bytes=60 * 1024 * 1024
        ),
        name="pfasst",
    )(velocity, start_field, guess)
    chunks = NXL // PLANES
    return pl.pallas_call(
        reorder,
        out_shape=jax.ShapeDtypeStruct((1, 3, NXL, NYL, NZL), F32),
        in_specs=[anywhere],
        out_specs=anywhere,
        scratch_shapes=[
            pltpu.VMEM((NXL * FP, 128), F32),
            pltpu.VMEM((2, 3, NXL, NYL, 128), F32),
            pltpu.SemaphoreType.DMA((chunks,)),
            pltpu.SemaphoreType.DMA((chunks, 2)),
        ],
        name="reorder",
    )(rows)


def solution(mesh):
    in_specs = (
        P(None, "gx", "gy", None),
        P(None, "gx", "gy", None),
        P("tm", None, "gx", "gy", None),
    )
    out_specs = P("tm", None, "gx", "gy", None)
    return jax.shard_map(shards, mesh=mesh, in_specs=in_specs, out_specs=out_specs, check_vma=False)
```

```python
import jax
import jax.numpy as jnp
from jax import lax
from jax.experimental import pallas as pl
from jax.experimental.pallas import tpu as pltpu
from jax.sharding import PartitionSpec as P


MESH = pl.DeviceIdType.MESH
F32 = jnp.float32
NU = 0.125
NUC = 0.03125
FP, CP = 192, 48
NXL, NYL, NZL = 16, 32, 256
NXC = NXL // 2
GUESS, START, NEXT, A1A, A2A, A1B, WRK, YB, VEL, A1P, WRKP, YBP, SUM = range(13)
NF = 13
CG, CSTART, CNEXT, CV2, CS1, CS2, CE1, CE2, CPS, CDX, CDY, CD0, CDXP, CDYP, CD0P = range(15)
NC = 15
XV, XG, XS, XCG, XCS, XS1, XE1, XA1, XA2, XCV2, XN, XCN, XS2, XE2, XB1, XW, XAP = range(17)
NX_ = 17
TE1, TE2, TZ, TU, TP, TPH, TG = range(7)
NT = TG + 4
PLANES = 4


def split3(v):
    hi = v.astype(jnp.bfloat16)
    rest = v - hi.astype(F32)
    mid = rest.astype(jnp.bfloat16)
    low = (rest - mid.astype(F32)).astype(jnp.bfloat16)
    return hi, mid, low


def permute(v, table):
    parts = [jnp.dot(p, table, preferred_element_type=F32) for p in split3(v)]
    return parts[0] + parts[1] + parts[2]


def kernel(vel_hbm, start_hbm, guess_hbm, out_hbm, raw, fb, gd, fh, fpk, cb, hvc, gc, ch, cpk, off, zin, zout,
           insem, outsem, xss, xrs, tss, trs):
    t, gx, gy = lax.axis_index("tm"), lax.axis_index("gx"), lax.axis_index("gy")
    first = t == 0
    gxm, gxp = lax.rem(gx + 7, 8), lax.rem(gx + 1, 8)
    gym, gyp = lax.rem(gy + 3, 4), lax.rem(gy + 1, 4)
    around = ((gxm, gy), (gxp, gy), (gx, gym), (gx, gyp))
    sub = lax.broadcasted_iota(jnp.int32, (2, 8, 128), 1)
    subc = lax.broadcasted_iota(jnp.int32, (8, 128), 0)
    row_i = lax.broadcasted_iota(jnp.int32, (256, 256), 0)
    col_i = lax.broadcasted_iota(jnp.int32, (256, 256), 1)

    def load(hbm, which):
        return [
            pltpu.make_async_copy(hbm.at[:, :, :, pl.ds(h * 128, 128)], raw.at[which, :, h], insem.at[which, h])
            for h in range(2)
        ]

    ins = [load(vel_hbm, 0), load(guess_hbm.at[0], 1), load(start_hbm, 2)]
    for copy in ins[0] + ins[1]:
        copy.start()

    @pl.when(first)
    def _():
        for copy in ins[2]:
            copy.start()

    bar = pltpu.get_barrier_semaphore()
    for ox, oy in around:
        pl.semaphore_signal(bar, inc=1, device_id=(t, ox, oy), device_id_type=MESH)

    @pl.when(t > 0)
    def _():
        pl.semaphore_signal(bar, inc=1, device_id=(t - 1, gx, gy), device_id_type=MESH)

    def exchange(src, dst, pack, halo, which, planes, size, dt=0):
        far = planes * size
        parts = (
            (src.at[pl.ds(size, size)], dst.at[pl.ds(far + size, size)]),
            (src.at[pl.ds(far, size)], dst.at[pl.ds(0, size)]),
            (pack.at[0], halo.at[1]),
            (pack.at[1], halo.at[0]),
        )
        return [
            pltpu.make_async_remote_copy(
                src_ref=s, dst_ref=d, send_sem=xss.at[which, i], recv_sem=xrs.at[which, i],
                device_id=(t + dt, around[i][0], around[i][1]), device_id_type=MESH)
            for i, (s, d) in enumerate(parts)
        ]

    def fine_exchange(k, which):
        return exchange(fb.at[k], fb.at[k], fpk.at[k], fh.at[k], which, NXL, FP)

    def coarse_exchange(k, dst, which, dt=0):
        return exchange(cb.at[k], cb.at[dst], cpk.at[k], ch.at[dst], which, NXC, CP, dt)

    def onward(src, dst, which):
        return pltpu.make_async_remote_copy(
            src_ref=src, dst_ref=dst, send_sem=tss.at[which], recv_sem=trs.at[which],
            device_id=(t + 1, gx, gy), device_id_type=MESH)

    def start(copies, which=(0, 1, 2, 3)):
        for i in which:
            copies[i].start()

    def arrive(copies, which=(0, 1, 2, 3)):
        for i in which:
            copies[i].wait_recv()

    def sent(copies):
        for copy in copies:
            copy.wait_send()

    def fine(k, plane, c, ym):
        return fb[k, pl.ds(pl.multiple_of(plane * FP + (c * 4 + ym) * 16, 16), 16), :].reshape(2, 8, 128)

    def put_fine(k, plane, c, ym, value):
        fb[k, pl.ds(pl.multiple_of(plane * FP + (c * 4 + ym) * 16, 16), 16), :] = value.reshape(16, 128)

    def coarse(k, plane, c, ym):
        return cb[k, pl.ds(pl.multiple_of(plane * CP + (c * 2 + ym) * 8, 8), 8), :]

    def put_coarse(k, plane, c, ym, value):
        cb[k, pl.ds(pl.multiple_of(plane * CP + (c * 2 + ym) * 8, 8), 8), :] = value

    def pack_fine(k):
        for c in range(3):
            for zm in range(2):
                for xm in range(2):
                    at = FP * (1 + xm) + c * 64 + zm * 8
                    to = ((c * 2 + zm) * 2 + xm) * 8
                    fpk[k, 0, pl.ds(to, 8), :] = fb[k, pl.ds(at, 8, stride=2 * FP), :]
                    fpk[k, 1, pl.ds(to, 8), :] = fb[k, pl.ds(at + 48 + 7, 8, stride=2 * FP), :]

    def pack_coarse(k):
        for c in range(3):
            at = CP + c * 16
            cpk[k, 0, pl.ds(c * 8, 8), :] = cb[k, pl.ds(at, 8, stride=CP), :]
            cpk[k, 1, pl.ds(c * 8, 8), :] = cb[k, pl.ds(at + 8 + 7, 8, stride=CP), :]

    def halo_rows(k, side, c, xs, xm):
        rows = [
            jnp.broadcast_to(fh[k, side, pl.ds(((c * 2 + zm) * 2 + xm) * 8 + xs, 1), :], (8, 128)) for zm in range(2)
        ]
        return jnp.stack(rows)

    def halo_row(k, side, c, x):
        return jnp.broadcast_to(ch[k, side, pl.ds(c * 8 + x, 1), :], (8, 128))

    def y_ahead(w, k, c, ym, xs, xm):
        if ym < 3:
            return w[ym + 1]
        if xm is None:
            return jnp.where(sub == 7, 0.0, pltpu.roll(w[0], 7, axis=1))
        return jnp.where(sub == 7, halo_rows(k, 1, c, xs, xm), pltpu.roll(w[0], 7, axis=1))

    def y_behind(w, k, c, ym, xs, xm):
        if ym > 0:
            return w[ym - 1]
        if xm is None:
            return jnp.where(sub == 0, 0.0, pltpu.roll(w[3], 1, axis=1))
        return jnp.where(sub == 0, halo_rows(k, 0, c, xs, xm), pltpu.roll(w[3], 1, axis=1))

    def z_ahead(v):
        return jnp.concatenate([v[1:2], pltpu.roll(v[0:1], 127, axis=2)], axis=0)

    def z_behind(v):
        return jnp.concatenate([pltpu.roll(v[1:2], 1, axis=2), v[0:1]], axis=0)

    def restricted(planes, ym):
        total = planes[0][2 * ym] + planes[0][2 * ym + 1] + planes[1][2 * ym] + planes[1][2 * ym + 1]
        return total[0] + total[1]

    def rhs(k, xs, xm, halo=True):
        x = 2 * xs + xm
        if not halo:
            xm = None
        w = [[fine(k, x + 1, c, ym) for ym in range(4)] for c in range(3)]
        out = [[None] * 4 for _ in range(3)]
        for ym in range(4):
            v = [fine(VEL, x + 1, b, ym) for b in range(3)]
            ahead = [NU - q for q in v]
            behind = [NU + q for q in v]
            for c in range(3):
                total = ahead[0] * fine(k, x + 2, c, ym) + behind[0] * fine(k, x, c, ym)
                total += ahead[1] * y_ahead(w[c], k, c, ym, xs, xm)
                total += behind[1] * y_behind(w[c], k, c, ym, xs, xm)
                total += ahead[2] * z_ahead(w[c][ym])
                total += behind[2] * z_behind(w[c][ym])
                for b in range(3):
                    at = x * (9 * 64) + ((3 * c + b) * 4 + ym) * 16
                    total += w[b][ym] * gd[pl.ds(pl.multiple_of(at, 16), 16), :].reshape(2, 8, 128)
                out[c][ym] = total
        return out

    def coarse_rhs(k, x):
        w = [[coarse(k, x + 1, c, ym) for ym in range(2)] for c in range(3)]
        out = [[None] * 2 for _ in range(3)]
        for ym in range(2):
            v = [hvc[pl.ds(pl.multiple_of(x * CP + (b * 2 + ym) * 8, 8), 8), :] for b in range(3)]
            ahead = [NUC - q for q in v]
            behind = [NUC + q for q in v]
            for c in range(3):
                if ym == 0:
                    ya = w[c][1]
                    yb = jnp.where(subc == 0, halo_row(k, 0, c, x), pltpu.roll(w[c][1], 1, axis=0))
                else:
                    ya = jnp.where(subc == 7, halo_row(k, 1, c, x), pltpu.roll(w[c][0], 7, axis=0))
                    yb = w[c][0]
                total = ahead[0] * coarse(k, x + 2, c, ym) + behind[0] * coarse(k, x, c, ym)
                total += ahead[1] * ya + behind[1] * yb
                total += ahead[2] * pltpu.roll(w[c][ym], 127, axis=1) + behind[2] * pltpu.roll(w[c][ym], 1, axis=1)
                for b in range(3):
                    at = x * 144 + ((3 * c + b) * 2 + ym) * 8
                    total += w[b][ym] * gc[pl.ds(pl.multiple_of(at, 8), 8), :]
                out[c][ym] = total
        return out

    def each(count, body, unroll=1):
        lax.fori_loop(0, count, lambda i, carry: (body(i), carry)[1], 0, unroll=unroll)

    def crow(x, c, ym):
        return pl.ds(pl.multiple_of(x * CP + (c * 2 + ym) * 8, 8), 8)

    def edges_first(i):
        return jnp.where(i == 0, 0, jnp.where(i == 1, NXC - 1, i - 1))

    def restricted_rhs(k, scale, use):
        def body(xs):
            planes = [rhs(k, xs, xm) for xm in range(2)]
            for c in range(3):
                for ym in range(2):
                    use(xs, c, ym, restricted([p[c] for p in planes], ym) * (scale / 8.0))

        each(NXC, body)

    table = (row_i == 2 * lax.rem(col_i, 128) + col_i // 128).astype(jnp.bfloat16)

    def take(read, k, c_from=0, c_to=3):
        def body(i):
            c, xq = i // 4, lax.rem(i, 4)
            got = permute(read(c, xq), table)
            for xx in range(4):
                for ym in range(4):
                    for zm in range(2):
                        at = (xq * 4 + xx + 1) * FP + c * 64 + (ym * 2 + zm) * 8
                        row = (xx * 4 + ym) * 8
                        fb[k, pl.ds(pl.multiple_of(at, 8), 8), :] = got[row : row + 8, zm * 128 : (zm + 1) * 128]

        lax.fori_loop(4 * c_from, 4 * c_to, lambda i, carry: (body(i), carry)[1], 0, unroll=2)

    def raw_rows(which):
        def read(c, xq):
            blocks = []
            for xx in range(4):
                for ym in range(4):
                    rows = [raw[which, c, h, xq * 4 + xx, pl.ds(ym, 8, stride=4), :] for h in range(2)]
                    blocks.append(jnp.concatenate(rows, axis=1))
            return jnp.concatenate(blocks, axis=0)

        return read

    def means(k, ck):
        def body(xs):
            for c in range(3):
                planes = [[fine(k, 2 * xs + xm + 1, c, ym) for ym in range(4)] for xm in range(2)]
                for ym in range(2):
                    put_coarse(ck, xs + 1, c, ym, restricted(planes, ym) * 0.125)

        each(NXC, body, 2)

    xv = fine_exchange(VEL, XV)
    xw = fine_exchange(SUM, XW)
    xg = fine_exchange(GUESS, XG)
    xs_ = fine_exchange(START, XS)
    xcg = coarse_exchange(CG, CG, XCG)

    guess_on = [
        onward(guess_hbm.at[0, 0, :, :, pl.ds(h * 128, 128)], raw.at[2, 0, h], TG + h) for h in range(2)
    ] + [onward(raw.at[1, c], raw.at[2, c], TG + 1 + c) for c in (1, 2)]

    @pl.when(t == 1)
    def _():
        pl.semaphore_wait(bar, 5)
        guess_on[0].start()
        guess_on[1].start()

    for k in (WRK, YB, WRKP, YBP):
        for plane in (0, NXL + 1):
            fb[k, pl.ds(plane * FP, FP), :] = jnp.zeros((FP, 128), F32)
    for copy in ins[0]:
        copy.wait()
    take(lambda c, xq: raw_rows(0)(c, xq) * 0.25, VEL)
    pack_fine(VEL)

    @pl.when(jnp.logical_or(t == 0, t == 2))
    def _():
        pl.semaphore_wait(bar, 5)

    @pl.when(t == 3)
    def _():
        pl.semaphore_wait(bar, 4)

    start(xv)
    for copy in ins[1]:
        copy.wait()
    @pl.when(first)
    def _():
        for copy in ins[2]:
            copy.wait()
        take(lambda c, xq: raw_rows(2)(c, xq) * (1.0 / 6.0) + raw_rows(1)(c, xq) * (5.0 / 6.0), SUM)
        pack_fine(SUM)
        start(xw)

    def take_guess():
        take(raw_rows(1), GUESS)
        pack_fine(GUESS)
        start(xg)
        means(GUESS, CG)
        pack_coarse(CG)
        start(xcg)

    @pl.when(t > 0)
    def _():
        take_guess()

    @pl.when(first)
    def _():
        take(raw_rows(2), START)
        means(START, CSTART)
        for side in range(2):
            ch[CSTART, side] = jnp.zeros((24, 128), F32)
            cb[CSTART, pl.ds(side * (NXC + 1) * CP, CP), :] = jnp.zeros((CP, 128), F32)

    arrive(xv)

    def gradients(xs):
        for a in range(3):
            kept = [[None, None] for _ in range(3)]
            vel = [None, None]
            for xm in range(2):
                x = 2 * xs + xm
                w = [fine(VEL, x + 1, a, ym) for ym in range(4)]
                vel[xm] = w
                diffs = [[None] * 4 for _ in range(3)]
                for ym in range(4):
                    diffs[0][ym] = fine(VEL, x + 2, a, ym) - fine(VEL, x, a, ym)
                    diffs[1][ym] = y_ahead(w, VEL, a, ym, xs, xm) - y_behind(w, VEL, a, ym, xs, xm)
                    diffs[2][ym] = z_ahead(w[ym]) - z_behind(w[ym])
                for b in range(3):
                    for ym in range(4):
                        if a == b:
                            diffs[b][ym] = diffs[b][ym] - 6.0 * NU
                        at = x * (9 * 64) + ((3 * a + b) * 4 + ym) * 16
                        gd[pl.ds(pl.multiple_of(at, 16), 16), :] = diffs[b][ym].reshape(16, 128)
                    kept[b][xm] = diffs[b]
            for ym in range(2):
                hvc[crow(xs, a, ym), :] = restricted(vel, ym) * 0.0625
                for b in range(3):
                    at = xs * 144 + ((3 * a + b) * 2 + ym) * 8
                    mean = restricted(kept[b], ym) * 0.125
                    if a == b:
                        mean = mean + 6.0 * (NU - NUC)
                    gc[pl.ds(pl.multiple_of(at, 8), 8), :] = mean

    each(NXC, gradients)

    @pl.when(first)
    def _():
        arrive(xw)

    @pl.when(t > 0)
    def _():
        arrive(xg)
        arrive(xcg)

    def keep_offset(x, c, ym, value):
        off[crow(x, c, ym), :] = value

    restricted_rhs(jnp.where(first, SUM, GUESS), 1.0, keep_offset)

    u0_1 = jnp.where(first, START, GUESS)
    u0_2 = jnp.where(first, START, NEXT)
    v0_1 = jnp.where(first, CSTART, CG)
    v0_2 = jnp.where(first, CSTART, CNEXT)
    s_1 = jnp.where(first, CSTART, CS1)
    s_2 = jnp.where(first, CSTART, CS2)

    @pl.when(t > 0)
    def _():
        def less_start(x):
            out = coarse_rhs(CG, x)
            for c in range(3):
                for ym in range(2):
                    at = crow(x, c, ym)
                    off[at, :] = off[at, :] - out[c][ym]

        each(NXC, less_start, 4)

    inner = pl.ds(CP, NXC * CP)

    def chain(ks, ke, xs_id, xe_id, te):
        to_next = onward(cb.at[ke, inner], cb.at[{CE1: CS1, CE2: CS2}[ke], inner], te)
        skew = coarse_exchange(ke, {CE1: CS1, CE2: CS2}[ke], xs_id, 1)
        same = coarse_exchange(ke, ke, xe_id)

        @pl.when(t > 0)
        def _():
            arrive(skew)
            to_next.wait_recv()

            def body(x):
                out = coarse_rhs(ks, x)
                for c in range(3):
                    for ym in range(2):
                        put_coarse(ke, x + 1, c, ym, coarse(ks, x + 1, c, ym) + out[c][ym] + off[crow(x, c, ym), :])

            each(NXC, body, 4)

        @pl.when(first)
        def _():
            def body(x):
                for c in range(3):
                    for ym in range(2):
                        put_coarse(ke, x + 1, c, ym, coarse(CSTART, x + 1, c, ym) + off[crow(x, c, ym), :])

            each(NXC, body, 4)

        pack_coarse(ke)

        @pl.when(t < 3)
        def _():
            start(skew)
            to_next.start()

        start(same)
        return to_next, skew, same

    xcs = coarse_exchange(CSTART, CSTART, XCS)

    @pl.when(t == 2)
    def _():
        for copy in guess_on[:2]:
            copy.wait_recv()
        take(raw_rows(2), START, 0, 1)

    next1, skew1, same1 = chain(CS1, CE1, XS1, XE1, TE1)

    before_on = [onward(cb.at[CS1], cb.at[CPS], TP), onward(ch.at[CS1], ch.at[CPS], TPH)]

    @pl.when(t == 1)
    def _():
        for copy in before_on:
            copy.start()

    @pl.when(first)
    def _():
        pack_fine(START)
        start(xs_)
        take_guess()
        arrive(xs_)
        arrive(xg)
        arrive(xcg)

        def keep(x, c, ym, value):
            zin[crow(x, c, ym), :] = value

        restricted_rhs(START, 1.0 / 6.0, keep)

    def give(xs):
        at = pl.ds(pl.multiple_of(xs * 2 * FP, 2 * FP), 2 * FP)
        return pltpu.make_async_copy(fb.at[WRK, pl.ds(pl.multiple_of(xs * 2 * FP + FP, FP), 2 * FP)], out_hbm.at[at], outsem.at[xs])

    def sweep(ku0, kv0, ks, kv2, ke, k1, k2, ka1, ka2, xa_id, halos_in, mean_of, kx=WRK, ky=YB, kdx=CDX, kdy=CDY, kd0=CD0):
        def corrections(x):
            for c in range(3):
                for ym in range(2):
                    d0 = coarse(ks, x, c, ym) - coarse(kv0, x, c, ym)
                    d2 = coarse(ke, x, c, ym) - coarse(kv2, x, c, ym)
                    put_coarse(kd0, x, c, ym, d0)
                    put_coarse(kdx, x, c, ym, 0.375 * d0 + 0.125 * d2)
                    put_coarse(kdy, x, c, ym, 0.125 * (d2 - d0))

        def x_of(u0, u1, u2, d):
            if k1 == k2:
                return (5.0 / 24.0) * u0 + (7.0 / 24.0) * u1 + d
            return (5.0 / 24.0) * u0 + (1.0 / 3.0) * u1 - (1.0 / 24.0) * u2 + d

        def y_of(a1, u0, u1, u2, d):
            if k1 == k2:
                return 0.5 * a1 - (1.0 / 24.0) * u0 + (1.0 / 24.0) * u1 + d
            return 0.5 * a1 - (1.0 / 24.0) * u0 - (1.0 / 6.0) * u1 + (5.0 / 24.0) * u2 + d

        def x_plane(i):
            p = i + 1
            xc = (p + 1) // 2
            for c in range(3):
                for ym in range(4):
                    d = coarse(kdx, xc, c, ym // 2)[None]
                    put_fine(kx, p, c, ym, x_of(fine(ku0, p, c, ym), fine(k1, p, c, ym), fine(k2, p, c, ym), d))

        xa = fine_exchange(ka1, xa_id)

        def first_node(xs):
            for xm in range(2):
                out = rhs(kx, xs, xm, False)
                p = 2 * xs + xm + 1
                for c in range(3):
                    for ym in range(4):
                        u0 = fine(ku0, p, c, ym)
                        a1 = u0 + coarse(kd0, xs + 1, c, ym // 2)[None] + out[c][ym]
                        put_fine(ka1, p, c, ym, a1)
                        d = coarse(kdy, xs + 1, c, ym // 2)[None]
                        put_fine(ky, p, c, ym, y_of(a1, u0, fine(k1, p, c, ym), fine(k2, p, c, ym), d))

        def second_node(xs):
            planes = []
            for xm in range(2):
                out = rhs(ky, xs, xm, False)
                p = 2 * xs + xm + 1
                for c in range(3):
                    for ym in range(4):
                        out[c][ym] = fine(ka1, p, c, ym) + out[c][ym]
                        put_fine(ka2, p, c, ym, out[c][ym])
                planes.append(out)
            if mean_of is not None:
                for c in range(3):
                    for ym in range(2):
                        put_coarse(mean_of, xs + 1, c, ym, restricted([q[c] for q in planes], ym) * 0.125)

        x_sides = ((0, 1, 0, 1), (NXL + 1, NXL, NXC + 1, NXC))

        def coefficient(side, v):
            return NU + v if side == 0 else NU - v

        def blocks(side):
            for c in range(3):
                for zm in range(2):
                    for xm in range(2):
                        at = FP * (1 + xm) + c * 64 + zm * 8 + side * 55
                        yield c, pl.ds(at, 8, stride=2 * FP), pl.ds(((c * 2 + zm) * 2 + xm) * 8, 8), pl.ds(((2 + zm) * 2 + xm) * 8, 8)

        def part1():
            each(NXC, lambda x: corrections(x + 1), 4)
            each(NXL, x_plane, 2)
            each(NXC, first_node)
            halos_in()
            for side, (far, edge, cfar, _) in enumerate(x_sides):
                corrections(cfar)
                for ym in range(4):
                    v = coefficient(side, fine(VEL, edge, 0, ym))
                    for c in range(3):
                        d = coarse(kdx, cfar, c, ym // 2)[None]
                        add = v * x_of(fine(ku0, far, c, ym), fine(k1, far, c, ym), fine(k2, far, c, ym), d)
                        put_fine(ka1, edge, c, ym, fine(ka1, edge, c, ym) + add)
                        put_fine(ky, edge, c, ym, fine(ky, edge, c, ym) + 0.5 * add)
            for side in range(2):
                d0 = ch[ks, side] - ch[kv0, side]
                d2 = ch[ke, side] - ch[kv2, side]
                ch[kdx, side] = 0.375 * d0 + 0.125 * d2
                ch[kdy, side] = 0.125 * (d2 - d0)
                for c, rows, at, vat in blocks(side):
                    d = ch[kdx, side, pl.ds(c * 8, 8), :]
                    far = x_of(fh[ku0, side, at, :], fh[k1, side, at, :], fh[k2, side, at, :], d)
                    add = coefficient(side, fpk[VEL, side, vat, :]) * far
                    value = fb[ka1, rows, :] + add
                    fb[ka1, rows, :] = value
                    fpk[ka1, side, at, :] = value
                    fb[ky, rows, :] = fb[ky, rows, :] + 0.5 * add
            start(xa)

        def part2():
            each(NXC, second_node)
            arrive(xa)
            for side, (far, edge, cfar, cedge) in enumerate(x_sides):
                adds = [[None] * 4 for _ in range(3)]
                for ym in range(4):
                    v = coefficient(side, fine(VEL, edge, 0, ym))
                    for c in range(3):
                        d = coarse(kdy, cfar, c, ym // 2)[None]
                        adds[c][ym] = v * y_of(fine(ka1, far, c, ym), fine(ku0, far, c, ym), fine(k1, far, c, ym), fine(k2, far, c, ym), d)
                        put_fine(ka2, edge, c, ym, fine(ka2, edge, c, ym) + adds[c][ym])
                if mean_of is not None:
                    for c in range(3):
                        for ym in range(2):
                            both = adds[c][2 * ym] + adds[c][2 * ym + 1]
                            put_coarse(mean_of, cedge, c, ym, coarse(mean_of, cedge, c, ym) + (both[0] + both[1]) * 0.125)
            for side in range(2):
                means_add = [None] * 3
                for c, rows, at, vat in blocks(side):
                    d = ch[kdy, side, pl.ds(c * 8, 8), :]
                    far = y_of(fh[ka1, side, at, :], fh[ku0, side, at, :], fh[k1, side, at, :], fh[k2, side, at, :], d)
                    add = coefficient(side, fpk[VEL, side, vat, :]) * far
                    value = fb[ka2, rows, :] + add
                    fb[ka2, rows, :] = value
                    fpk[ka2, side, at, :] = value
                    means_add[c] = add if means_add[c] is None else means_add[c] + add
                if mean_of is not None:
                    for c in range(3):
                        rows = pl.ds(CP + c * 16 + side * 15, 8, stride=CP)
                        value = cb[mean_of, rows, :] + means_add[c] * 0.125
                        cb[mean_of, rows, :] = value
                        cpk[mean_of, side, pl.ds(c * 8, 8), :] = value

        return xa, part1, part2

    xa2 = fine_exchange(A2A, XA2)
    xcv2 = coarse_exchange(CV2, CV2, XCV2)
    xn = fine_exchange(NEXT, XN)
    xcn = coarse_exchange(CNEXT, CNEXT, XCN)

    def before_in():
        arrive(xs_)
        arrive(xcs)

    xa1, own1, own2 = sweep(u0_1, v0_1, s_1, CG, CE1, GUESS, GUESS, A1A, A2A, XA1, lambda: arrive(same1), CV2)
    xap, before1, before2 = sweep(START, CSTART, CPS, CSTART, CS1, START, START, A1P, NEXT, XAP, before_in, CNEXT,
                                  WRKP, YBP, CDXP, CDYP, CD0P)
    own1()

    @pl.when(t == 1)
    def _():
        guess_on[2].start()

    own2()
    start(xa2)
    start(xcv2)

    @pl.when(t == 1)
    def _():
        guess_on[3].start()

    @pl.when(t == 2)
    def _():
        for copy in guess_on[2:]:
            copy.wait_recv()
        take(raw_rows(2), START, 1, 3)
        pack_fine(START)
        start(xs_)
        means(START, CSTART)
        pack_coarse(CSTART)
        start(xcs)
        for copy in before_on:
            copy.wait_recv()
        before1()

    whole = pl.ds(FP, NXL * FP)
    bulk = onward(fb.at[A2A, whole], fb.at[NEXT, whole], TU)
    to_z = onward(zout, zin, TZ)
    even = jnp.logical_or(t == 0, t == 2)
    odd = jnp.logical_or(t == 1, t == 3)

    @pl.when(even)
    def _():
        bulk.start()

    restricted_rhs(A1A, 2.0 / 3.0, keep_offset)
    arrive(xa2)
    arrive(xcv2)

    def both(x, c, ym, value):
        at = crow(x, c, ym)
        off[at, :] = off[at, :] + value
        zout[at, :] = value

    restricted_rhs(A2A, 1.0 / 6.0, both)

    def less_end(x):
        out = coarse_rhs(CV2, x)
        for c in range(3):
            for ym in range(2):
                at = crow(x, c, ym)
                zout[at, :] = zout[at, :] - out[c][ym]

    each(NXC, less_end, 4)

    @pl.when(t < 3)
    def _():
        to_z.start()

    @pl.when(t > 0)
    def _():
        to_z.wait_recv()

    def add_previous(x):
        for c in range(3):
            for ym in range(2):
                at = crow(x, c, ym)
                off[at, :] = off[at, :] + zin[at, :]

    each(NXC, add_previous, 4)
    next2, skew2, same2 = chain(CS2, CE2, XS2, XE2, TE2)

    @pl.when(t == 2)
    def _():
        before2()
        start(xn)
        start(xcn)

    @pl.when(odd)
    def _():
        bulk.wait_recv()
        start(xn, (0, 1))
        pack_fine(NEXT)
        start(xn, (2, 3))
        means(NEXT, CNEXT)
        pack_coarse(CNEXT)
        start(xcn)

    def second_in():
        arrive(same2)

        @pl.when(t > 0)
        def _():
            arrive(xn)
            arrive(xcn)

    xb1, own1, own2 = sweep(u0_2, v0_2, s_2, CV2, CE2, A1A, A2A, A1B, WRK, XB1, second_in, None)
    own1()
    own2()
    for xs in range(NXC):
        give(xs).start()

    for copies in (xv, xg, xcg, same1, xa1, xa2, xcv2, same2, xb1):
        sent(copies)

    @pl.when(first)
    def _():
        sent(xw)

    @pl.when(even)
    def _():
        sent(xs_)
        sent([bulk])

    @pl.when(t == 1)
    def _():
        sent(guess_on + before_on)

    @pl.when(t == 2)
    def _():
        sent(xcs)
        sent(xap)

    @pl.when(t > 0)
    def _():
        sent(xn)
        sent(xcn)

    @pl.when(t < 3)
    def _():
        for copies in (skew1, skew2, [next1, next2, to_z]):
            sent(copies)

    for xs in range(NXC):
        give(xs).wait()


def reorder(rows_hbm, out_hbm, rows, halves, insem, outsem):
    chunks = NXL // PLANES
    size = PLANES * FP

    def get(i):
        at = pl.ds(i * size, size)
        return pltpu.make_async_copy(rows_hbm.at[at], rows.at[at], insem.at[i])

    def put(i, h):
        return pltpu.make_async_copy(
            halves.at[h, :, pl.ds(i * PLANES, PLANES)],
            out_hbm.at[0, :, pl.ds(i * PLANES, PLANES), :, pl.ds(h * 128, 128)], outsem.at[i, h])

    for i in range(chunks):
        get(i).start()
    row_i = lax.broadcasted_iota(jnp.int32, (256, 256), 0)
    col_i = lax.broadcasted_iota(jnp.int32, (256, 256), 1)
    back = (col_i == 2 * lax.rem(row_i, 128) + row_i // 128).astype(jnp.bfloat16)
    for i in range(chunks):
        get(i).wait()
        for c in range(3):
            blocks = []
            for xx in range(PLANES):
                for ym in range(4):
                    at = i * size + xx * FP + (c * 4 + ym) * 16
                    blocks.append(jnp.concatenate([rows[pl.ds(at + 8 * zm, 8), :] for zm in range(2)], axis=1))
            got = permute(jnp.concatenate(blocks, axis=0), back)
            for xx in range(PLANES):
                for ym in range(4):
                    row = (xx * 4 + ym) * 8
                    for h in range(2):
                        halves[h, c, i * PLANES + xx, pl.ds(ym, 8, stride=4), :] = got[row : row + 8, h * 128 : (h + 1) * 128]
        for h in range(2):
            put(i, h).start()
    for i in range(chunks):
        for h in range(2):
            put(i, h).wait()


def shards(velocity, start_field, guess):
    anywhere = pl.BlockSpec(memory_space=pl.ANY)
    rows = pl.pallas_call(
        kernel,
        out_shape=jax.ShapeDtypeStruct((NXL * FP, 128), F32),
        in_specs=[anywhere] * 3,
        out_specs=anywhere,
        scratch_shapes=[
            pltpu.VMEM((3, 3, 2, NXL, NYL, 128), F32),
            pltpu.VMEM((NF, (NXL + 2) * FP, 128), F32),
            pltpu.VMEM((NXL * 9 * 64, 128), F32),
            pltpu.VMEM((NF, 2, 96, 128), F32),
            pltpu.VMEM((NF, 2, 96, 128), F32),
            pltpu.VMEM((NC, (NXC + 2) * CP, 128), F32),
            pltpu.VMEM((NXC * CP, 128), F32),
            pltpu.VMEM((NXC * 144, 128), F32),
            pltpu.VMEM((NC, 2, 24, 128), F32),
            pltpu.VMEM((NC, 2, 24, 128), F32),
            pltpu.VMEM((NXC * CP, 128), F32),
            pltpu.VMEM((NXC * CP, 128), F32),
            pltpu.VMEM((NXC * CP, 128), F32),
            pltpu.SemaphoreType.DMA((3, 2)),
            pltpu.SemaphoreType.DMA((NXC,)),
            pltpu.SemaphoreType.DMA((NX_, 4)),
            pltpu.SemaphoreType.DMA((NX_, 4)),
            pltpu.SemaphoreType.DMA((NT,)),
            pltpu.SemaphoreType.DMA((NT,)),
        ],
        compiler_params=pltpu.CompilerParams(
            collective_id=0, has_side_effects=True, vmem_limit_bytes=60 * 1024 * 1024
        ),
        name="pfasst",
    )(velocity, start_field, guess)
    chunks = NXL // PLANES
    return pl.pallas_call(
        reorder,
        out_shape=jax.ShapeDtypeStruct((1, 3, NXL, NYL, NZL), F32),
        in_specs=[anywhere],
        out_specs=anywhere,
        scratch_shapes=[
            pltpu.VMEM((NXL * FP, 128), F32),
            pltpu.VMEM((2, 3, NXL, NYL, 128), F32),
            pltpu.SemaphoreType.DMA((chunks,)),
            pltpu.SemaphoreType.DMA((chunks, 2)),
        ],
        name="reorder",
    )(rows)


def solution(mesh):
    in_specs = (
        P(None, "gx", "gy", None),
        P(None, "gx", "gy", None),
        P("tm", None, "gx", "gy", None),
    )
    out_specs = P("tm", None, "gx", "gy", None)
    return jax.shard_map(shards, mesh=mesh, in_specs=in_specs, out_specs=out_specs, check_vma=False)
```

```python
import jax
import jax.numpy as jnp
from jax import lax
from jax.experimental import pallas as pl
from jax.experimental.pallas import tpu as pltpu
from jax.sharding import PartitionSpec as P


MESH = pl.DeviceIdType.MESH
F32 = jnp.float32
NU = 0.125
NUC = 0.03125
FP, CP = 192, 48
NXL, NYL, NZL = 16, 32, 256
NXC = NXL // 2
GUESS, START, NEXT, A1A, A2A, A1B, WRK, YB, VEL, A1P, WRKP, YBP, SUM = range(13)
NF = 13
CG, CSTART, CNEXT, CV2, CS1, CS2, CE1, CE2, CPS, CDX, CDY, CD0, CDXP, CDYP, CD0P = range(15)
NC = 15
XV, XG, XS, XCG, XCS, XS1, XE1, XA1, XA2, XCV2, XN, XCN, XS2, XE2, XB1, XW, XAP = range(17)
NX_ = 17
TE1, TE2, TZ, TU, TP, TPH, TG = range(7)
NT = TG + 4
PLANES = 4


def split3(v):
    hi = v.astype(jnp.bfloat16)
    rest = v - hi.astype(F32)
    mid = rest.astype(jnp.bfloat16)
    low = (rest - mid.astype(F32)).astype(jnp.bfloat16)
    return hi, mid, low


def permute(v, table):
    parts = [jnp.dot(p, table, preferred_element_type=F32) for p in split3(v)]
    return parts[0] + parts[1] + parts[2]


def kernel(vel_hbm, start_hbm, guess_hbm, out_hbm, raw, fb, gd, fh, fpk, cb, hvc, gc, ch, cpk, off, zin, zout,
           insem, outsem, xss, xrs, tss, trs):
    t, gx, gy = lax.axis_index("tm"), lax.axis_index("gx"), lax.axis_index("gy")
    first = t == 0
    gxm, gxp = lax.rem(gx + 7, 8), lax.rem(gx + 1, 8)
    gym, gyp = lax.rem(gy + 3, 4), lax.rem(gy + 1, 4)
    around = ((gxm, gy), (gxp, gy), (gx, gym), (gx, gyp))
    sub = lax.broadcasted_iota(jnp.int32, (2, 8, 128), 1)
    subc = lax.broadcasted_iota(jnp.int32, (8, 128), 0)
    row_i = lax.broadcasted_iota(jnp.int32, (256, 256), 0)
    col_i = lax.broadcasted_iota(jnp.int32, (256, 256), 1)

    def load(hbm, which):
        return [
            pltpu.make_async_copy(hbm.at[:, :, :, pl.ds(h * 128, 128)], raw.at[which, :, h], insem.at[which, h])
            for h in range(2)
        ]

    ins = [load(vel_hbm, 0), load(guess_hbm.at[0], 1), load(start_hbm, 2)]
    for copy in ins[0] + ins[1]:
        copy.start()

    @pl.when(first)
    def _():
        for copy in ins[2]:
            copy.start()

    bar = pltpu.get_barrier_semaphore()
    for ox, oy in around:
        pl.semaphore_signal(bar, inc=1, device_id=(t, ox, oy), device_id_type=MESH)

    @pl.when(t > 0)
    def _():
        pl.semaphore_signal(bar, inc=1, device_id=(t - 1, gx, gy), device_id_type=MESH)

    def exchange(src, dst, pack, halo, which, planes, size, dt=0):
        far = planes * size
        parts = (
            (src.at[pl.ds(size, size)], dst.at[pl.ds(far + size, size)]),
            (src.at[pl.ds(far, size)], dst.at[pl.ds(0, size)]),
            (pack.at[0], halo.at[1]),
            (pack.at[1], halo.at[0]),
        )
        return [
            pltpu.make_async_remote_copy(
                src_ref=s, dst_ref=d, send_sem=xss.at[which, i], recv_sem=xrs.at[which, i],
                device_id=(t + dt, around[i][0], around[i][1]), device_id_type=MESH)
            for i, (s, d) in enumerate(parts)
        ]

    def fine_exchange(k, which):
        return exchange(fb.at[k], fb.at[k], fpk.at[k], fh.at[k], which, NXL, FP)

    def coarse_exchange(k, dst, which, dt=0):
        return exchange(cb.at[k], cb.at[dst], cpk.at[k], ch.at[dst], which, NXC, CP, dt)

    def onward(src, dst, which):
        return pltpu.make_async_remote_copy(
            src_ref=src, dst_ref=dst, send_sem=tss.at[which], recv_sem=trs.at[which],
            device_id=(t + 1, gx, gy), device_id_type=MESH)

    def start(copies, which=(0, 1, 2, 3)):
        for i in which:
            copies[i].start()

    def arrive(copies, which=(0, 1, 2, 3)):
        for i in which:
            copies[i].wait_recv()

    def sent(copies):
        for copy in copies:
            copy.wait_send()

    def fine(k, plane, c, ym):
        return fb[k, pl.ds(pl.multiple_of(plane * FP + (c * 4 + ym) * 16, 16), 16), :].reshape(2, 8, 128)

    def put_fine(k, plane, c, ym, value):
        fb[k, pl.ds(pl.multiple_of(plane * FP + (c * 4 + ym) * 16, 16), 16), :] = value.reshape(16, 128)

    def coarse(k, plane, c, ym):
        return cb[k, pl.ds(pl.multiple_of(plane * CP + (c * 2 + ym) * 8, 8), 8), :]

    def put_coarse(k, plane, c, ym, value):
        cb[k, pl.ds(pl.multiple_of(plane * CP + (c * 2 + ym) * 8, 8), 8), :] = value

    def pack_fine(k):
        for c in range(3):
            for zm in range(2):
                for xm in range(2):
                    at = FP * (1 + xm) + c * 64 + zm * 8
                    to = ((c * 2 + zm) * 2 + xm) * 8
                    fpk[k, 0, pl.ds(to, 8), :] = fb[k, pl.ds(at, 8, stride=2 * FP), :]
                    fpk[k, 1, pl.ds(to, 8), :] = fb[k, pl.ds(at + 48 + 7, 8, stride=2 * FP), :]

    def pack_coarse(k):
        for c in range(3):
            at = CP + c * 16
            cpk[k, 0, pl.ds(c * 8, 8), :] = cb[k, pl.ds(at, 8, stride=CP), :]
            cpk[k, 1, pl.ds(c * 8, 8), :] = cb[k, pl.ds(at + 8 + 7, 8, stride=CP), :]

    def halo_rows(k, side, c, xs, xm):
        rows = [
            jnp.broadcast_to(fh[k, side, pl.ds(((c * 2 + zm) * 2 + xm) * 8 + xs, 1), :], (8, 128)) for zm in range(2)
        ]
        return jnp.stack(rows)

    def halo_row(k, side, c, x):
        return jnp.broadcast_to(ch[k, side, pl.ds(c * 8 + x, 1), :], (8, 128))

    def y_ahead(w, k, c, ym, xs, xm):
        if ym < 3:
            return w[ym + 1]
        if xm is None:
            return jnp.where(sub == 7, 0.0, pltpu.roll(w[0], 7, axis=1))
        return jnp.where(sub == 7, halo_rows(k, 1, c, xs, xm), pltpu.roll(w[0], 7, axis=1))

    def y_behind(w, k, c, ym, xs, xm):
        if ym > 0:
            return w[ym - 1]
        if xm is None:
            return jnp.where(sub == 0, 0.0, pltpu.roll(w[3], 1, axis=1))
        return jnp.where(sub == 0, halo_rows(k, 0, c, xs, xm), pltpu.roll(w[3], 1, axis=1))

    def z_ahead(v):
        return jnp.concatenate([v[1:2], pltpu.roll(v[0:1], 127, axis=2)], axis=0)

    def z_behind(v):
        return jnp.concatenate([pltpu.roll(v[1:2], 1, axis=2), v[0:1]], axis=0)

    def restricted(planes, ym):
        total = planes[0][2 * ym] + planes[0][2 * ym + 1] + planes[1][2 * ym] + planes[1][2 * ym + 1]
        return total[0] + total[1]

    def rhs(k, xs, xm, halo=True):
        x = 2 * xs + xm
        if not halo:
            xm = None
        w = [[fine(k, x + 1, c, ym) for ym in range(4)] for c in range(3)]
        out = [[None] * 4 for _ in range(3)]
        for ym in range(4):
            v = [fine(VEL, x + 1, b, ym) for b in range(3)]
            ahead = [NU - q for q in v]
            behind = [NU + q for q in v]
            for c in range(3):
                total = ahead[0] * fine(k, x + 2, c, ym) + behind[0] * fine(k, x, c, ym)
                total += ahead[1] * y_ahead(w[c], k, c, ym, xs, xm)
                total += behind[1] * y_behind(w[c], k, c, ym, xs, xm)
                total += ahead[2] * z_ahead(w[c][ym])
                total += behind[2] * z_behind(w[c][ym])
                for b in range(3):
                    at = x * (9 * 64) + ((3 * c + b) * 4 + ym) * 16
                    total += w[b][ym] * gd[pl.ds(pl.multiple_of(at, 16), 16), :].reshape(2, 8, 128)
                out[c][ym] = total
        return out

    def coarse_rhs(k, x):
        w = [[coarse(k, x + 1, c, ym) for ym in range(2)] for c in range(3)]
        out = [[None] * 2 for _ in range(3)]
        for ym in range(2):
            v = [hvc[pl.ds(pl.multiple_of(x * CP + (b * 2 + ym) * 8, 8), 8), :] for b in range(3)]
            ahead = [NUC - q for q in v]
            behind = [NUC + q for q in v]
            for c in range(3):
                if ym == 0:
                    ya = w[c][1]
                    yb = jnp.where(subc == 0, halo_row(k, 0, c, x), pltpu.roll(w[c][1], 1, axis=0))
                else:
                    ya = jnp.where(subc == 7, halo_row(k, 1, c, x), pltpu.roll(w[c][0], 7, axis=0))
                    yb = w[c][0]
                total = ahead[0] * coarse(k, x + 2, c, ym) + behind[0] * coarse(k, x, c, ym)
                total += ahead[1] * ya + behind[1] * yb
                total += ahead[2] * pltpu.roll(w[c][ym], 127, axis=1) + behind[2] * pltpu.roll(w[c][ym], 1, axis=1)
                for b in range(3):
                    at = x * 144 + ((3 * c + b) * 2 + ym) * 8
                    total += w[b][ym] * gc[pl.ds(pl.multiple_of(at, 8), 8), :]
                out[c][ym] = total
        return out

    def each(count, body, unroll=1):
        lax.fori_loop(0, count, lambda i, carry: (body(i), carry)[1], 0, unroll=unroll)

    def crow(x, c, ym):
        return pl.ds(pl.multiple_of(x * CP + (c * 2 + ym) * 8, 8), 8)

    def edges_last(i):
        return jnp.where(i == NXC - 2, 0, jnp.where(i == NXC - 1, NXC - 1, i + 1))

    def restricted_rhs(k, scale, use, x_halo=None):
        def body(i):
            xs = edges_last(i)
            if x_halo is not None:
                pl.when(i == NXC - 2)(x_halo)
            planes = [rhs(k, xs, xm) for xm in range(2)]
            for c in range(3):
                for ym in range(2):
                    use(xs, c, ym, restricted([p[c] for p in planes], ym) * (scale / 8.0))

        each(NXC, body)

    table = (row_i == 2 * lax.rem(col_i, 128) + col_i // 128).astype(jnp.bfloat16)

    def take(read, k, c_from=0, c_to=3):
        def body(i):
            c, xq = i // 4, lax.rem(i, 4)
            got = permute(read(c, xq), table)
            for xx in range(4):
                for ym in range(4):
                    for zm in range(2):
                        at = (xq * 4 + xx + 1) * FP + c * 64 + (ym * 2 + zm) * 8
                        row = (xx * 4 + ym) * 8
                        fb[k, pl.ds(pl.multiple_of(at, 8), 8), :] = got[row : row + 8, zm * 128 : (zm + 1) * 128]

        lax.fori_loop(4 * c_from, 4 * c_to, lambda i, carry: (body(i), carry)[1], 0, unroll=2)

    def raw_rows(which):
        def read(c, xq):
            blocks = []
            for xx in range(4):
                for ym in range(4):
                    rows = [raw[which, c, h, xq * 4 + xx, pl.ds(ym, 8, stride=4), :] for h in range(2)]
                    blocks.append(jnp.concatenate(rows, axis=1))
            return jnp.concatenate(blocks, axis=0)

        return read

    def means(k, ck):
        def body(xs):
            for c in range(3):
                planes = [[fine(k, 2 * xs + xm + 1, c, ym) for ym in range(4)] for xm in range(2)]
                for ym in range(2):
                    put_coarse(ck, xs + 1, c, ym, restricted(planes, ym) * 0.125)

        each(NXC, body, 2)

    xv = fine_exchange(VEL, XV)
    xw = fine_exchange(SUM, XW)
    xg = fine_exchange(GUESS, XG)
    xs_ = fine_exchange(START, XS)
    xcg = coarse_exchange(CG, CG, XCG)

    guess_on = [
        onward(guess_hbm.at[0, 0, :, :, pl.ds(h * 128, 128)], raw.at[2, 0, h], TG + h) for h in range(2)
    ] + [onward(raw.at[1, c], raw.at[2, c], TG + 1 + c) for c in (1, 2)]

    @pl.when(t == 1)
    def _():
        pl.semaphore_wait(bar, 5)
        guess_on[0].start()
        guess_on[1].start()

    for k in (WRK, YB, WRKP, YBP):
        for plane in (0, NXL + 1):
            fb[k, pl.ds(plane * FP, FP), :] = jnp.zeros((FP, 128), F32)
    for copy in ins[0]:
        copy.wait()
    take(lambda c, xq: raw_rows(0)(c, xq) * 0.25, VEL)
    pack_fine(VEL)

    @pl.when(jnp.logical_or(t == 0, t == 2))
    def _():
        pl.semaphore_wait(bar, 5)

    @pl.when(t == 3)
    def _():
        pl.semaphore_wait(bar, 4)

    start(xv)
    for copy in ins[1]:
        copy.wait()
    @pl.when(first)
    def _():
        for copy in ins[2]:
            copy.wait()
        take(lambda c, xq: raw_rows(2)(c, xq) * (1.0 / 6.0) + raw_rows(1)(c, xq) * (5.0 / 6.0), SUM)
        pack_fine(SUM)
        start(xw)

    def take_guess():
        take(raw_rows(1), GUESS)
        pack_fine(GUESS)
        start(xg)
        means(GUESS, CG)
        pack_coarse(CG)
        start(xcg)

    @pl.when(t > 0)
    def _():
        take_guess()

    @pl.when(first)
    def _():
        take(raw_rows(2), START)
        means(START, CSTART)
        for side in range(2):
            ch[CSTART, side] = jnp.zeros((24, 128), F32)
            cb[CSTART, pl.ds(side * (NXC + 1) * CP, CP), :] = jnp.zeros((CP, 128), F32)

    arrive(xv, (2, 3))

    def gradients(i):
        xs = edges_last(i)
        pl.when(i == NXC - 2)(lambda: arrive(xv, (0, 1)))
        for a in range(3):
            kept = [[None, None] for _ in range(3)]
            vel = [None, None]
            for xm in range(2):
                x = 2 * xs + xm
                w = [fine(VEL, x + 1, a, ym) for ym in range(4)]
                vel[xm] = w
                diffs = [[None] * 4 for _ in range(3)]
                for ym in range(4):
                    diffs[0][ym] = fine(VEL, x + 2, a, ym) - fine(VEL, x, a, ym)
                    diffs[1][ym] = y_ahead(w, VEL, a, ym, xs, xm) - y_behind(w, VEL, a, ym, xs, xm)
                    diffs[2][ym] = z_ahead(w[ym]) - z_behind(w[ym])
                for b in range(3):
                    for ym in range(4):
                        if a == b:
                            diffs[b][ym] = diffs[b][ym] - 6.0 * NU
                        at = x * (9 * 64) + ((3 * a + b) * 4 + ym) * 16
                        gd[pl.ds(pl.multiple_of(at, 16), 16), :] = diffs[b][ym].reshape(16, 128)
                    kept[b][xm] = diffs[b]
            for ym in range(2):
                hvc[crow(xs, a, ym), :] = restricted(vel, ym) * 0.0625
                for b in range(3):
                    at = xs * 144 + ((3 * a + b) * 2 + ym) * 8
                    mean = restricted(kept[b], ym) * 0.125
                    if a == b:
                        mean = mean + 6.0 * (NU - NUC)
                    gc[pl.ds(pl.multiple_of(at, 8), 8), :] = mean

    each(NXC, gradients)

    def sum_in(which):
        pl.when(first)(lambda: arrive(xw, which))
        pl.when(t > 0)(lambda: arrive(xg, which))

    sum_in((2, 3))

    def keep_offset(x, c, ym, value):
        off[crow(x, c, ym), :] = value

    restricted_rhs(jnp.where(first, SUM, GUESS), 1.0, keep_offset, lambda: sum_in((0, 1)))

    u0_1 = jnp.where(first, START, GUESS)
    u0_2 = jnp.where(first, START, NEXT)
    v0_1 = jnp.where(first, CSTART, CG)
    v0_2 = jnp.where(first, CSTART, CNEXT)
    s_1 = jnp.where(first, CSTART, CS1)
    s_2 = jnp.where(first, CSTART, CS2)

    @pl.when(t > 0)
    def _():
        arrive(xcg)

        def less_start(x):
            out = coarse_rhs(CG, x)
            for c in range(3):
                for ym in range(2):
                    at = crow(x, c, ym)
                    off[at, :] = off[at, :] - out[c][ym]

        each(NXC, less_start, 4)

    inner = pl.ds(CP, NXC * CP)

    def chain(ks, ke, xs_id, xe_id, te):
        to_next = onward(cb.at[ke, inner], cb.at[{CE1: CS1, CE2: CS2}[ke], inner], te)
        skew = coarse_exchange(ke, {CE1: CS1, CE2: CS2}[ke], xs_id, 1)
        same = coarse_exchange(ke, ke, xe_id)

        @pl.when(t > 0)
        def _():
            arrive(skew)
            to_next.wait_recv()

            def body(x):
                out = coarse_rhs(ks, x)
                for c in range(3):
                    for ym in range(2):
                        put_coarse(ke, x + 1, c, ym, coarse(ks, x + 1, c, ym) + out[c][ym] + off[crow(x, c, ym), :])

            each(NXC, body, 4)

        @pl.when(first)
        def _():
            def body(x):
                for c in range(3):
                    for ym in range(2):
                        put_coarse(ke, x + 1, c, ym, coarse(CSTART, x + 1, c, ym) + off[crow(x, c, ym), :])

            each(NXC, body, 4)

        pack_coarse(ke)

        @pl.when(t < 3)
        def _():
            start(skew)
            to_next.start()

        start(same)
        return to_next, skew, same

    xcs = coarse_exchange(CSTART, CSTART, XCS)

    @pl.when(t == 2)
    def _():
        for copy in guess_on[:2]:
            copy.wait_recv()
        take(raw_rows(2), START, 0, 1)

    next1, skew1, same1 = chain(CS1, CE1, XS1, XE1, TE1)

    before_on = [onward(cb.at[CS1], cb.at[CPS], TP), onward(ch.at[CS1], ch.at[CPS], TPH)]

    @pl.when(t == 1)
    def _():
        for copy in before_on:
            copy.start()

    @pl.when(first)
    def _():
        pack_fine(START)
        start(xs_)
        take_guess()
        arrive(xs_)
        arrive(xg)
        arrive(xcg)

        def keep(x, c, ym, value):
            zin[crow(x, c, ym), :] = value

        restricted_rhs(START, 1.0 / 6.0, keep)

    def give(xs):
        at = pl.ds(pl.multiple_of(xs * 2 * FP, 2 * FP), 2 * FP)
        return pltpu.make_async_copy(fb.at[WRK, pl.ds(pl.multiple_of(xs * 2 * FP + FP, FP), 2 * FP)], out_hbm.at[at], outsem.at[xs])

    def sweep(ku0, kv0, ks, kv2, ke, k1, k2, ka1, ka2, xa_id, halos_in, mean_of, kx=WRK, ky=YB, kdx=CDX, kdy=CDY, kd0=CD0):
        def corrections(x):
            for c in range(3):
                for ym in range(2):
                    d0 = coarse(ks, x, c, ym) - coarse(kv0, x, c, ym)
                    d2 = coarse(ke, x, c, ym) - coarse(kv2, x, c, ym)
                    put_coarse(kd0, x, c, ym, d0)
                    put_coarse(kdx, x, c, ym, 0.375 * d0 + 0.125 * d2)
                    put_coarse(kdy, x, c, ym, 0.125 * (d2 - d0))

        def x_of(u0, u1, u2, d):
            if k1 == k2:
                return (5.0 / 24.0) * u0 + (7.0 / 24.0) * u1 + d
            return (5.0 / 24.0) * u0 + (1.0 / 3.0) * u1 - (1.0 / 24.0) * u2 + d

        def y_of(a1, u0, u1, u2, d):
            if k1 == k2:
                return 0.5 * a1 - (1.0 / 24.0) * u0 + (1.0 / 24.0) * u1 + d
            return 0.5 * a1 - (1.0 / 24.0) * u0 - (1.0 / 6.0) * u1 + (5.0 / 24.0) * u2 + d

        def x_plane(i):
            p = i + 1
            xc = (p + 1) // 2
            for c in range(3):
                for ym in range(4):
                    d = coarse(kdx, xc, c, ym // 2)[None]
                    put_fine(kx, p, c, ym, x_of(fine(ku0, p, c, ym), fine(k1, p, c, ym), fine(k2, p, c, ym), d))

        xa = fine_exchange(ka1, xa_id)

        def first_node(xs):
            for xm in range(2):
                out = rhs(kx, xs, xm, False)
                p = 2 * xs + xm + 1
                for c in range(3):
                    for ym in range(4):
                        u0 = fine(ku0, p, c, ym)
                        a1 = u0 + coarse(kd0, xs + 1, c, ym // 2)[None] + out[c][ym]
                        put_fine(ka1, p, c, ym, a1)
                        d = coarse(kdy, xs + 1, c, ym // 2)[None]
                        put_fine(ky, p, c, ym, y_of(a1, u0, fine(k1, p, c, ym), fine(k2, p, c, ym), d))

        def second_node(xs):
            planes = []
            for xm in range(2):
                out = rhs(ky, xs, xm, False)
                p = 2 * xs + xm + 1
                for c in range(3):
                    for ym in range(4):
                        out[c][ym] = fine(ka1, p, c, ym) + out[c][ym]
                        put_fine(ka2, p, c, ym, out[c][ym])
                planes.append(out)
            if mean_of is not None:
                for c in range(3):
                    for ym in range(2):
                        put_coarse(mean_of, xs + 1, c, ym, restricted([q[c] for q in planes], ym) * 0.125)

        x_sides = ((0, 1, 0, 1), (NXL + 1, NXL, NXC + 1, NXC))

        def coefficient(side, v):
            return NU + v if side == 0 else NU - v

        def blocks(side):
            for c in range(3):
                for zm in range(2):
                    for xm in range(2):
                        at = FP * (1 + xm) + c * 64 + zm * 8 + side * 55
                        yield c, pl.ds(at, 8, stride=2 * FP), pl.ds(((c * 2 + zm) * 2 + xm) * 8, 8), pl.ds(((2 + zm) * 2 + xm) * 8, 8)

        def part1():
            each(NXC, lambda x: corrections(x + 1), 4)
            each(NXL, x_plane, 2)
            each(NXC, first_node)
            halos_in()
            for side, (far, edge, cfar, _) in enumerate(x_sides):
                corrections(cfar)
                for ym in range(4):
                    v = coefficient(side, fine(VEL, edge, 0, ym))
                    for c in range(3):
                        d = coarse(kdx, cfar, c, ym // 2)[None]
                        add = v * x_of(fine(ku0, far, c, ym), fine(k1, far, c, ym), fine(k2, far, c, ym), d)
                        put_fine(ka1, edge, c, ym, fine(ka1, edge, c, ym) + add)
                        put_fine(ky, edge, c, ym, fine(ky, edge, c, ym) + 0.5 * add)
            for side in range(2):
                d0 = ch[ks, side] - ch[kv0, side]
                d2 = ch[ke, side] - ch[kv2, side]
                ch[kdx, side] = 0.375 * d0 + 0.125 * d2
                ch[kdy, side] = 0.125 * (d2 - d0)
                for c, rows, at, vat in blocks(side):
                    d = ch[kdx, side, pl.ds(c * 8, 8), :]
                    far = x_of(fh[ku0, side, at, :], fh[k1, side, at, :], fh[k2, side, at, :], d)
                    add = coefficient(side, fpk[VEL, side, vat, :]) * far
                    value = fb[ka1, rows, :] + add
                    fb[ka1, rows, :] = value
                    fpk[ka1, side, at, :] = value
                    fb[ky, rows, :] = fb[ky, rows, :] + 0.5 * add
            start(xa)

        def part2():
            each(NXC, second_node)
            arrive(xa)
            for side, (far, edge, cfar, cedge) in enumerate(x_sides):
                adds = [[None] * 4 for _ in range(3)]
                for ym in range(4):
                    v = coefficient(side, fine(VEL, edge, 0, ym))
                    for c in range(3):
                        d = coarse(kdy, cfar, c, ym // 2)[None]
                        adds[c][ym] = v * y_of(fine(ka1, far, c, ym), fine(ku0, far, c, ym), fine(k1, far, c, ym), fine(k2, far, c, ym), d)
                        put_fine(ka2, edge, c, ym, fine(ka2, edge, c, ym) + adds[c][ym])
                if mean_of is not None:
                    for c in range(3):
                        for ym in range(2):
                            both = adds[c][2 * ym] + adds[c][2 * ym + 1]
                            put_coarse(mean_of, cedge, c, ym, coarse(mean_of, cedge, c, ym) + (both[0] + both[1]) * 0.125)
            for side in range(2):
                means_add = [None] * 3
                for c, rows, at, vat in blocks(side):
                    d = ch[kdy, side, pl.ds(c * 8, 8), :]
                    far = y_of(fh[ka1, side, at, :], fh[ku0, side, at, :], fh[k1, side, at, :], fh[k2, side, at, :], d)
                    add = coefficient(side, fpk[VEL, side, vat, :]) * far
                    value = fb[ka2, rows, :] + add
                    fb[ka2, rows, :] = value
                    fpk[ka2, side, at, :] = value
                    means_add[c] = add if means_add[c] is None else means_add[c] + add
                if mean_of is not None:
                    for c in range(3):
                        rows = pl.ds(CP + c * 16 + side * 15, 8, stride=CP)
                        value = cb[mean_of, rows, :] + means_add[c] * 0.125
                        cb[mean_of, rows, :] = value
                        cpk[mean_of, side, pl.ds(c * 8, 8), :] = value

        return xa, part1, part2

    xa2 = fine_exchange(A2A, XA2)
    xcv2 = coarse_exchange(CV2, CV2, XCV2)
    xn = fine_exchange(NEXT, XN)
    xcn = coarse_exchange(CNEXT, CNEXT, XCN)

    def before_in():
        arrive(xs_)
        arrive(xcs)

    xa1, own1, own2 = sweep(u0_1, v0_1, s_1, CG, CE1, GUESS, GUESS, A1A, A2A, XA1, lambda: arrive(same1), CV2)
    xap, before1, before2 = sweep(START, CSTART, CPS, CSTART, CS1, START, START, A1P, NEXT, XAP, before_in, CNEXT,
                                  WRKP, YBP, CDXP, CDYP, CD0P)
    own1()

    @pl.when(t == 1)
    def _():
        guess_on[2].start()

    own2()
    start(xa2)
    start(xcv2)

    @pl.when(t == 1)
    def _():
        guess_on[3].start()

    @pl.when(t == 2)
    def _():
        for copy in guess_on[2:]:
            copy.wait_recv()
        take(raw_rows(2), START, 1, 3)
        pack_fine(START)
        start(xs_)
        means(START, CSTART)
        pack_coarse(CSTART)
        start(xcs)
        for copy in before_on:
            copy.wait_recv()
        before1()

    whole = pl.ds(FP, NXL * FP)
    bulk = onward(fb.at[A2A, whole], fb.at[NEXT, whole], TU)
    to_z = onward(zout, zin, TZ)
    even = jnp.logical_or(t == 0, t == 2)
    odd = jnp.logical_or(t == 1, t == 3)

    @pl.when(even)
    def _():
        bulk.start()

    restricted_rhs(A1A, 2.0 / 3.0, keep_offset)
    arrive(xa2, (2, 3))

    def both(x, c, ym, value):
        at = crow(x, c, ym)
        off[at, :] = off[at, :] + value
        zout[at, :] = value

    restricted_rhs(A2A, 1.0 / 6.0, both, lambda: arrive(xa2, (0, 1)))
    arrive(xcv2)

    def less_end(x):
        out = coarse_rhs(CV2, x)
        for c in range(3):
            for ym in range(2):
                at = crow(x, c, ym)
                zout[at, :] = zout[at, :] - out[c][ym]

    each(NXC, less_end, 4)

    @pl.when(t < 3)
    def _():
        to_z.start()

    @pl.when(t > 0)
    def _():
        to_z.wait_recv()

    def add_previous(x):
        for c in range(3):
            for ym in range(2):
                at = crow(x, c, ym)
                off[at, :] = off[at, :] + zin[at, :]

    each(NXC, add_previous, 4)
    next2, skew2, same2 = chain(CS2, CE2, XS2, XE2, TE2)

    @pl.when(t == 2)
    def _():
        before2()
        start(xn)
        start(xcn)

    @pl.when(odd)
    def _():
        bulk.wait_recv()
        start(xn, (0, 1))
        pack_fine(NEXT)
        start(xn, (2, 3))
        means(NEXT, CNEXT)
        pack_coarse(CNEXT)
        start(xcn)

    def second_in():
        arrive(same2)

        @pl.when(t > 0)
        def _():
            arrive(xn)
            arrive(xcn)

    xb1, own1, own2 = sweep(u0_2, v0_2, s_2, CV2, CE2, A1A, A2A, A1B, WRK, XB1, second_in, None)
    own1()
    own2()
    for xs in range(NXC):
        give(xs).start()

    for copies in (xv, xg, xcg, same1, xa1, xa2, xcv2, same2, xb1):
        sent(copies)

    @pl.when(first)
    def _():
        sent(xw)

    @pl.when(even)
    def _():
        sent(xs_)
        sent([bulk])

    @pl.when(t == 1)
    def _():
        sent(guess_on + before_on)

    @pl.when(t == 2)
    def _():
        sent(xcs)
        sent(xap)

    @pl.when(t > 0)
    def _():
        sent(xn)
        sent(xcn)

    @pl.when(t < 3)
    def _():
        for copies in (skew1, skew2, [next1, next2, to_z]):
            sent(copies)

    for xs in range(NXC):
        give(xs).wait()


def reorder(rows_hbm, out_hbm, rows, halves, insem, outsem):
    chunks = NXL // PLANES
    size = PLANES * FP

    def get(i):
        at = pl.ds(i * size, size)
        return pltpu.make_async_copy(rows_hbm.at[at], rows.at[at], insem.at[i])

    def put(i, h):
        return pltpu.make_async_copy(
            halves.at[h, :, pl.ds(i * PLANES, PLANES)],
            out_hbm.at[0, :, pl.ds(i * PLANES, PLANES), :, pl.ds(h * 128, 128)], outsem.at[i, h])

    for i in range(chunks):
        get(i).start()
    row_i = lax.broadcasted_iota(jnp.int32, (256, 256), 0)
    col_i = lax.broadcasted_iota(jnp.int32, (256, 256), 1)
    back = (col_i == 2 * lax.rem(row_i, 128) + row_i // 128).astype(jnp.bfloat16)
    for i in range(chunks):
        get(i).wait()
        for c in range(3):
            blocks = []
            for xx in range(PLANES):
                for ym in range(4):
                    at = i * size + xx * FP + (c * 4 + ym) * 16
                    blocks.append(jnp.concatenate([rows[pl.ds(at + 8 * zm, 8), :] for zm in range(2)], axis=1))
            got = permute(jnp.concatenate(blocks, axis=0), back)
            for xx in range(PLANES):
                for ym in range(4):
                    row = (xx * 4 + ym) * 8
                    for h in range(2):
                        halves[h, c, i * PLANES + xx, pl.ds(ym, 8, stride=4), :] = got[row : row + 8, h * 128 : (h + 1) * 128]
        for h in range(2):
            put(i, h).start()
    for i in range(chunks):
        for h in range(2):
            put(i, h).wait()


def shards(velocity, start_field, guess):
    anywhere = pl.BlockSpec(memory_space=pl.ANY)
    rows = pl.pallas_call(
        kernel,
        out_shape=jax.ShapeDtypeStruct((NXL * FP, 128), F32),
        in_specs=[anywhere] * 3,
        out_specs=anywhere,
        scratch_shapes=[
            pltpu.VMEM((3, 3, 2, NXL, NYL, 128), F32),
            pltpu.VMEM((NF, (NXL + 2) * FP, 128), F32),
            pltpu.VMEM((NXL * 9 * 64, 128), F32),
            pltpu.VMEM((NF, 2, 96, 128), F32),
            pltpu.VMEM((NF, 2, 96, 128), F32),
            pltpu.VMEM((NC, (NXC + 2) * CP, 128), F32),
            pltpu.VMEM((NXC * CP, 128), F32),
            pltpu.VMEM((NXC * 144, 128), F32),
            pltpu.VMEM((NC, 2, 24, 128), F32),
            pltpu.VMEM((NC, 2, 24, 128), F32),
            pltpu.VMEM((NXC * CP, 128), F32),
            pltpu.VMEM((NXC * CP, 128), F32),
            pltpu.VMEM((NXC * CP, 128), F32),
            pltpu.SemaphoreType.DMA((3, 2)),
            pltpu.SemaphoreType.DMA((NXC,)),
            pltpu.SemaphoreType.DMA((NX_, 4)),
            pltpu.SemaphoreType.DMA((NX_, 4)),
            pltpu.SemaphoreType.DMA((NT,)),
            pltpu.SemaphoreType.DMA((NT,)),
        ],
        compiler_params=pltpu.CompilerParams(
            collective_id=0, has_side_effects=True, vmem_limit_bytes=60 * 1024 * 1024
        ),
        name="pfasst",
    )(velocity, start_field, guess)
    chunks = NXL // PLANES
    return pl.pallas_call(
        reorder,
        out_shape=jax.ShapeDtypeStruct((1, 3, NXL, NYL, NZL), F32),
        in_specs=[anywhere],
        out_specs=anywhere,
        scratch_shapes=[
            pltpu.VMEM((NXL * FP, 128), F32),
            pltpu.VMEM((2, 3, NXL, NYL, 128), F32),
            pltpu.SemaphoreType.DMA((chunks,)),
            pltpu.SemaphoreType.DMA((chunks, 2)),
        ],
        name="reorder",
    )(rows)


def solution(mesh):
    in_specs = (
        P(None, "gx", "gy", None),
        P(None, "gx", "gy", None),
        P("tm", None, "gx", "gy", None),
    )
    out_specs = P("tm", None, "gx", "gy", None)
    return jax.shard_map(shards, mesh=mesh, in_specs=in_specs, out_specs=out_specs, check_vma=False)
```
